256 devices in a mesh: lon: 32 (over z, x_lo, core), lat: 8 (over x_hi, y).
Axes of the slice: x: 4 (x_hi: 2, x_lo: 2; x = x_hi * 2 + x_lo), y: 4, z: 8, core: 2. Of those that a mesh axis runs over, the one named last changes fastest.
Arguments:
- potential_heat: float32 [8, 1024, 4096], P(None, 'lat', 'lon'), may hold values from -6 to 6
- saltiness_anomaly: float32 [8, 1024, 4096], P(None, 'lat', 'lon'), may hold values from -6 to 6
- east_current: float32 [8, 1024, 4096], P(None, 'lat', 'lon'), may hold values from -1 to 1
- north_current: float32 [8, 1024, 4096], P(None, 'lat', 'lon'), may hold values from -1 to 1
- water_indicator: int32 [8, 1024, 4096], P(None, 'lat', 'lon'), may hold values from 0 to 1, as said below
- east_west_courant_factor: float32 [1024, 4096], P('lat', 'lon'), may hold values from 0.05 to 0.45
- north_south_courant_factor: float32 [1024, 4096], P('lat', 'lon'), may hold values from 0.05 to 0.45
- interface_diffusion_factor: float32 [7, 1024, 4096], P(None, 'lat', 'lon'), may hold values from 0.05 to 5
- spreading_coefficient: float32 [4, 8], replicated, may hold values from 0.05 to 0.25
- seam_mirror_index: int32 [4096], P('lon'), may hold values from 0 to 4095, as said below
Outputs:
- temperature_next: float32 [8, 1024, 4096], P(None, 'lat', 'lon')
- salinity_next: float32 [8, 1024, 4096], P(None, 'lat', 'lon')
- zonal_next: float32 [8, 1024, 4096], P(None, 'lat', 'lon')
- meridional_next: float32 [8, 1024, 4096], P(None, 'lat', 'lon')
The draws below stay inside these ranges and needn't reach their ends.
Inputs may be any that keep to these rules, and one draw needn't show every extreme that they name: water_indicator is 0 or 1, and a cell below a land cell is land. seam_mirror_index[i] = (p - i) mod 4096 for one p whose remainder on division by 128 is 127.
All inputs are finite; a program needn't handle non-finite values.
Results may differ from the reference program's by a relative error of at most 0.0003.
Values sent between devices are 32-bit elements; how exact they have to be, the bound alone decides.
No kernel may reach another device: no remote copies, remote signals or barrier semaphores. Data moves between devices by JAX's collectives and lax.ppermute only.
A program may use at most 128 MiB of HBM per device.

```python
import math
import jax
import jax.numpy as jnp
from jax import lax

SLAB_LAYERS = 8
COLS = 128
PARALLEL_LINES = 1024
MERIDIAN_LINES = 4096


def draw_water_indicator(key, part):
    column_depth = jax.random.randint(key, (PARALLEL_LINES, MERIDIAN_LINES), -1, SLAB_LAYERS + 1)
    column_depth = jnp.maximum(column_depth, 0)
    level_index = jnp.arange(SLAB_LAYERS, dtype=jnp.int32)[:, None, None]
    return (level_index < column_depth[None]).astype(jnp.int32)


def draw_seam_mirror_index(key, part):
    tile_count = MERIDIAN_LINES // COLS
    tile_pick = jax.random.randint(jax.random.fold_in(key, 7), (), 0, tile_count)
    fold_pivot = tile_pick * COLS + COLS - 1
    columns = jnp.arange(MERIDIAN_LINES, dtype=jnp.int32)
    return ((fold_pivot - columns) % MERIDIAN_LINES).astype(jnp.int32)


def steps_of(rng, extent, cuts, low, largest):
    gain, own = 1.0, jax.random.fold_in(rng, 6)
    for axis_at, blocks in cuts:
        steps = jnp.exp(jax.random.uniform(jax.random.fold_in(own, axis_at), (blocks,), jnp.float32, low / len(cuts), largest / len(cuts)))
        gain = gain * jnp.repeat(steps, extent[axis_at] // blocks).reshape([-1 if axis == axis_at else 1 for axis in range(len(extent))])
    return gain


def bell_draw(stream_key, shape, scale, most, split=(), kind=jnp.bfloat16):
    drawn = scale * jax.random.normal(stream_key, shape, jnp.float32)
    if split:
        drawn = drawn * steps_of(stream_key, shape, split, -0.22, 0.18)
    return jnp.clip(drawn, -most, most).astype(kind)


def setup_inputs(seed: int = 0) -> dict:
    seeds = jax.random.split(jax.random.key(seed), 11)
    potential_heat = bell_draw(seeds[0], (SLAB_LAYERS, PARALLEL_LINES, MERIDIAN_LINES), 1.0, 6.0, ((1, 8), (2, 32)), jnp.float32)
    saltiness_anomaly = bell_draw(seeds[1], (SLAB_LAYERS, PARALLEL_LINES, MERIDIAN_LINES), 1.0, 6.0, ((1, 8), (2, 32)), jnp.float32)
    east_current = jnp.clip(jax.random.uniform(seeds[2], (SLAB_LAYERS, PARALLEL_LINES, MERIDIAN_LINES), jnp.float32, -1.0, 1.0) * steps_of(seeds[2], (SLAB_LAYERS, PARALLEL_LINES, MERIDIAN_LINES), ((1, 8), (2, 32)), -0.4, 0.0), -1.0, 1.0)
    north_current = jnp.clip(jax.random.uniform(seeds[3], (SLAB_LAYERS, PARALLEL_LINES, MERIDIAN_LINES), jnp.float32, -1.0, 1.0) * steps_of(seeds[3], (SLAB_LAYERS, PARALLEL_LINES, MERIDIAN_LINES), ((1, 8), (2, 32)), -0.4, 0.0), -1.0, 1.0)
    water_indicator = draw_water_indicator(jax.random.fold_in(seeds[10], 71), 0)
    east_west_courant_factor = jnp.clip(jnp.exp(math.log(0.45) - 2.1972245 * jax.random.uniform(seeds[5], (PARALLEL_LINES, MERIDIAN_LINES), jnp.float32) ** steps_of(seeds[5], (PARALLEL_LINES, MERIDIAN_LINES), ((0, 8), (1, 32)), -0.2, 0.2)), 0.05, 0.45)
    north_south_courant_factor = jnp.clip(jnp.exp(math.log(0.45) - 2.1972245 * jax.random.uniform(seeds[6], (PARALLEL_LINES, MERIDIAN_LINES), jnp.float32) ** steps_of(seeds[6], (PARALLEL_LINES, MERIDIAN_LINES), ((0, 8), (1, 32)), -0.2, 0.2)), 0.05, 0.45)
    interface_diffusion_factor = jnp.clip(jnp.exp(math.log(5.0) - 4.6051702 * jax.random.uniform(seeds[7], (SLAB_LAYERS - 1, PARALLEL_LINES, MERIDIAN_LINES), jnp.float32) ** steps_of(seeds[7], (SLAB_LAYERS - 1, PARALLEL_LINES, MERIDIAN_LINES), ((1, 8), (2, 32)), -0.2, 0.2)), 0.05, 5.0)
    spreading_coefficient = jnp.clip(jax.random.uniform(seeds[8], (4, SLAB_LAYERS), jnp.float32, 0.05, 0.25), 0.05, 0.25)
    seam_mirror_index = draw_seam_mirror_index(jax.random.fold_in(seeds[10], 71), 0)
    return dict(potential_heat=potential_heat, saltiness_anomaly=saltiness_anomaly, east_current=east_current, north_current=north_current, water_indicator=water_indicator, east_west_courant_factor=east_west_courant_factor, north_south_courant_factor=north_south_courant_factor, interface_diffusion_factor=interface_diffusion_factor, spreading_coefficient=spreading_coefficient, seam_mirror_index=seam_mirror_index)


def cut(source, first_index, last_index, dimension):
    return lax.slice_in_dim(source, first_index, last_index, axis=dimension)


def ppm_update(extended, courant, opening, dimension):
    length = extended.shape[dimension] - 6
    edge_value = (7.0 / 12.0) * (cut(extended, 1, length + 4, dimension) + cut(extended, 2, length + 5, dimension)) - (1.0 / 12.0) * (cut(extended, 0, length + 3, dimension) + cut(extended, 3, length + 6, dimension))
    left_edge = cut(edge_value, 0, length + 2, dimension)
    right_edge = cut(edge_value, 1, length + 3, dimension)
    centre = cut(extended, 2, length + 4, dimension)
    slopes = right_edge - left_edge
    curvature = 6.0 * (centre - 0.5 * (left_edge + right_edge))
    courant_size = jnp.abs(courant)
    shape_factor = 1.0 - (2.0 / 3.0) * courant_size
    from_left = cut(right_edge, 0, length + 1, dimension) - 0.5 * courant_size * (cut(slopes, 0, length + 1, dimension) - shape_factor * cut(curvature, 0, length + 1, dimension))
    from_right = cut(left_edge, 1, length + 2, dimension) + 0.5 * courant_size * (cut(slopes, 1, length + 2, dimension) + shape_factor * cut(curvature, 1, length + 2, dimension))
    fluxes = courant * opening * jnp.where(courant >= 0.0, from_left, from_right)
    return cut(fluxes, 0, length, dimension) - cut(fluxes, 1, length + 1, dimension)


def face_terms(speed_metric, wet_ext, metric_ext, dimension):
    length = wet_ext.shape[dimension] - 6
    courant = 0.5 * (cut(speed_metric, 2, length + 3, dimension) + cut(speed_metric, 3, length + 4, dimension))
    opening = cut(wet_ext, 2, length + 3, dimension) * cut(wet_ext, 3, length + 4, dimension)
    weight = 0.5 * (cut(metric_ext, 2, length + 3, dimension) + cut(metric_ext, 3, length + 4, dimension)) * opening
    return courant, opening, weight


def vertical_solve(target_rhs, coupling):
    layer_total = target_rhs.shape[1]
    zeros_plane = jnp.zeros_like(target_rhs[:, 0])
    factors = []
    reduced = []
    for layer_index in range(layer_total):
        upward = coupling[layer_index - 1] if layer_index > 0 else zeros_plane
        downward = coupling[layer_index] if layer_index < layer_total - 1 else zeros_plane
        divisor = 1.0 + upward + downward
        target = target_rhs[:, layer_index]
        if layer_index > 0:
            divisor = divisor - upward * factors[layer_index - 1]
            target = target + upward * reduced[layer_index - 1]
        factors.append(downward / divisor)
        reduced.append(target / divisor)
    solved_levels = [reduced[layer_total - 1]]
    for layer_index in range(layer_total - 2, -1, -1):
        solved_levels.insert(0, reduced[layer_index] + factors[layer_index] * solved_levels[0])
    return jnp.stack(solved_levels, axis=1)


def lon_extend(source, width):
    return jnp.concatenate([source[..., -width:], source, source[..., :width]], axis=2)


def lat_extend(source, width, sign_value, seam_mirror_index):
    lower_rows = jnp.zeros_like(source[:, :width, :])
    top_rows = source[:, source.shape[1] - width:, :][:, ::-1, :]
    upper_rows = sign_value * jnp.take(top_rows, seam_mirror_index, axis=2)
    return jnp.concatenate([lower_rows, source, upper_rows], axis=1)


def reference(potential_heat, saltiness_anomaly, east_current, north_current, water_indicator, east_west_courant_factor, north_south_courant_factor, interface_diffusion_factor, spreading_coefficient, seam_mirror_index):
    ocean_point_indicator = water_indicator.astype(jnp.float32)
    transported_quantities = [potential_heat * ocean_point_indicator, saltiness_anomaly * ocean_point_indicator, east_current * ocean_point_indicator, north_current * ocean_point_indicator]
    sign_list = [1.0, 1.0, -1.0, -1.0]
    zonal_row = east_west_courant_factor[None]
    merid_row = north_south_courant_factor[None]
    wet_x = lon_extend(ocean_point_indicator, 3)
    metric_x = lon_extend(zonal_row, 3)
    speed_x = lon_extend(transported_quantities[2], 3) * metric_x
    courant_x, opening_x, weight_x = face_terms(speed_x, wet_x, metric_x, 2)
    starred = [one_field + ppm_update(lon_extend(one_field, 3), courant_x, opening_x, 2) for one_field in transported_quantities]
    wet_y = lat_extend(ocean_point_indicator, 3, 1.0, seam_mirror_index)
    metric_y = lat_extend(merid_row, 3, 1.0, seam_mirror_index)
    speed_y = lat_extend(transported_quantities[3], 3, -1.0, seam_mirror_index) * metric_y
    courant_y, opening_y, weight_y = face_terms(speed_y, wet_y, metric_y, 1)
    advected = [starred[field_index] + ppm_update(lat_extend(starred[field_index], 3, sign_list[field_index], seam_mirror_index), courant_y, opening_y, 1) for field_index in range(4)]
    coupling = interface_diffusion_factor * ocean_point_indicator[:-1] * ocean_point_indicator[1:]
    results = []
    for field_index in range(4):
        one_field = advected[field_index]
        wide_stack = lon_extend(one_field, 1)
        tall_stack = lat_extend(one_field, 1, sign_list[field_index], seam_mirror_index)
        laplacian = weight_x[:, :, 1:] * (wide_stack[:, :, 2:] - one_field) - weight_x[:, :, :-1] * (one_field - wide_stack[:, :, :-2]) + weight_y[:, 1:, :] * (tall_stack[:, 2:, :] - one_field) - weight_y[:, :-1, :] * (one_field - tall_stack[:, :-2, :])
        diffused = one_field + spreading_coefficient[field_index][:, None, None] * laplacian
        solved = vertical_solve(diffused[None], coupling)[0]
        results.append(solved * ocean_point_indicator)
    return (results[0], results[1], results[2], results[3])
```

```python
import functools
import jax
import jax.numpy as jnp
from jax import lax
from jax.experimental import pallas as pl
from jax.experimental.pallas import tpu as pltpu
from jax.sharding import PartitionSpec as P

F32 = jnp.float32
LEVELS = 8
TILE = 8
LANES = 128
VM, DEPTH, METRIC, STRIP, VM_S, DEPTH_S, METRIC_S, PLANES = 32, 40, 41, 42, 44, 45, 46, 47
PAIRS = 24
AD_STRIP, WY, AD_PLANES = 32, 34, 42


def roll(x, shift):
    shift %= LANES
    return x if shift == 0 else pltpu.roll(x, shift, 1)


def turn(x, shift):
    return pltpu.roll(x, shift % TILE, 0)


def iota(dimension):
    return lax.broadcasted_iota(jnp.int32, (TILE, LANES), dimension)


def face_coefs(courant):
    size = jnp.abs(courant)
    rest = 1.0 - size
    edge = courant * rest * (1.0 / 12.0)
    return edge * rest, courant * size * (3.0 - 2.0 * size), edge * size, courant >= 0.0


def edge_sum(before, here, after, beyond):
    return 7.0 * (here + after) - (before + beyond)


def flux_of(coefs, here, after, edge, edge_before, edge_after):
    own, centre, far, positive = coefs
    return own * edge + centre * jnp.where(positive, here, after) - far * jnp.where(positive, edge_before, edge_after)


def pack_kernel(t_ref, s_ref, u_ref, v_ref, w_ref, mx_ref, my_ref, own_ref, ownx_ref, toe_ref, tow_ref):
    fields = (t_ref, s_ref, u_ref, v_ref)
    rows_total = mx_ref.shape[0]
    lane = iota(1)
    low = (lane & 7) < 4
    group = lane >> 3
    zero = jnp.zeros((TILE, LANES), F32)
    for i in range(3):
        ownx_ref[i] = zero

    def body(t, carry):
        rows = pl.ds(pl.multiple_of(t * TILE, TILE), TILE)
        wet = [w_ref[l, rows, :] for l in range(LEVELS)]
        depth = sum(wet[1:], wet[0]).astype(F32)
        packs = []
        for k in range(2):
            pack = zero
            for p in range(16):
                q = jnp.where(wet[p % 8] != 0, fields[2 * k + p // 8][p % 8, rows, :], 0.0)
                pack = jnp.where(group == p, roll(q, 4 + 8 * p), pack)
            packs.append(pack)
            own_ref[k, rows, :] = pack
        toe_ref[rows, :] = jnp.where(low, packs[0], roll(packs[1], 4))
        tow_ref[rows, :] = jnp.where(low, roll(packs[1], -4), packs[0])
        shift = (4 + 8 * t) & (LANES - 1)
        for i, x in enumerate((depth, mx_ref[rows, :], my_ref[rows, :])):
            ownx_ref[i] = jnp.where(group == t, pltpu.roll(x, shift, 1), ownx_ref[i])
        return carry

    lax.fori_loop(0, rows_total // TILE, body, 0)
    depth, metric_x, metric_y = ownx_ref[0], ownx_ref[1], ownx_ref[2]
    first, second = pl.ds(rows_total, TILE), pl.ds(rows_total + TILE, TILE)
    toe_ref[first, :] = jnp.where(low, depth, roll(metric_x, 4))
    toe_ref[second, :] = jnp.where(low, metric_y, 0.0)
    tow_ref[first, :] = jnp.where(low, roll(metric_x, -4), depth)
    tow_ref[second, :] = jnp.where(low, 0.0, metric_y)


def x_tile(t, fields, w_ref, mx_ref, my_ref, own_ref, ownx_ref, fromw_ref, frome_ref, put, put_weight):
    rows_total = mx_ref.shape[0]
    start = t * TILE if isinstance(t, int) else pl.multiple_of(t * TILE, TILE)
    rows = pl.ds(start, TILE)
    lane = iota(1)
    low = (lane & 7) < 4
    group = lane >> 3
    level = (group & 7).astype(F32)
    half = lane < 64
    west, east = fromw_ref[rows, :], frome_ref[rows, :]
    halo = (jnp.where(low, west, east), jnp.where(low, roll(west, -4), roll(east, 4)))
    own = (own_ref[0, rows, :], own_ref[1, rows, :])
    strips = [(jnp.where(low, halo[k], own[k]), jnp.where(low, own[k], halo[k])) for k in range(2)]
    first, second = pl.ds(rows_total, TILE), pl.ds(rows_total + TILE, TILE)
    west, east = fromw_ref[first, :], frome_ref[first, :]
    west_2, east_2 = fromw_ref[second, :], frome_ref[second, :]
    side_halo = (
        jnp.where(low, west, east),
        jnp.where(low, roll(west, -4), roll(east, 4)),
        jnp.where(low, west_2, east_2),
    )

    def spread(x):
        x = jnp.where(group == t, x, 0.0)
        for shift in (8, 16, 32, 64):
            x = x + roll(x, shift)
        return x

    extra = []
    for i in range(3):
        mine = ownx_ref[i]
        extra.append((spread(jnp.where(low, side_halo[i], mine)), spread(jnp.where(low, mine, side_halo[i]))))
    depth_s, mx_s, my_s = extra

    um_s, weight_s, edge_s, flux_s, star_s, vm_s = [], [], [[], []], [[], []], [[], []], []
    for side in range(2):
        mixed = strips[1][side]
        swapped = roll(mixed, 64)
        um = jnp.where(half, mixed, swapped) * mx_s[side]
        vm_s.append(jnp.where(half, swapped, mixed) * my_s[side])
        opening = jnp.minimum(depth_s[side], roll(depth_s[side], -1)) > level
        coefs = face_coefs(jnp.where(opening, 0.5 * (um + roll(um, -1)), 0.0))
        um_s.append(um)
        weight_s.append(jnp.where(opening, 0.5 * (mx_s[side] + roll(mx_s[side], -1)), 0.0))
        for k in range(2):
            q = strips[k][side]
            after = roll(q, -1)
            edge = edge_sum(roll(q, 1), q, after, roll(q, -2))
            flux = flux_of(coefs, q, after, edge, roll(edge, 1), roll(edge, -1))
            edge_s[k].append(edge)
            flux_s[k].append(flux)
            star_s[k].append(q + roll(flux, 1) - flux)
    um_halo = jnp.where(low, um_s[0], um_s[1])
    edge_halo = [jnp.where(low, edge_s[k][0], edge_s[k][1]) for k in range(2)]
    for k in range(2):
        put(STRIP + k, jnp.where(low, star_s[k][0], star_s[k][1]))
    put(VM_S, jnp.where(low, vm_s[0], vm_s[1]))
    put(DEPTH_S, jnp.where(low, depth_s[0], depth_s[1]))
    put(METRIC_S, jnp.where(low, my_s[0], my_s[1]))

    head, tail, heads = lane == 0, lane == LANES - 1, lane < 2
    wet = [w_ref[l, rows, :] for l in range(LEVELS)]
    depth = sum(wet[1:], wet[0]).astype(F32)
    mx, my = mx_ref[rows, :], my_ref[rows, :]
    put(DEPTH, depth)
    put(METRIC, my)
    shallow = jnp.minimum(depth, roll(jnp.where(head, roll(depth_s[1], -4), depth), -1))
    mean_metric = 0.5 * (mx + roll(jnp.where(head, roll(mx_s[1], -4), mx), -1))
    for l in range(LEVELS):
        masked = [jnp.where(wet[l] != 0, field[l, rows, :], 0.0) for field in fields]
        um = masked[2] * mx
        put(VM + l, masked[3] * my)
        opening = shallow > float(l)
        place = 124 - 8 * l
        coefs = face_coefs(
            jnp.where(opening, 0.5 * (um + roll(jnp.where(head, roll(um_halo, place), um), -1)), 0.0)
        )
        if put_weight is not None:
            weight = jnp.where(opening, mean_metric, 0.0)
            put_weight(l, weight)
            put_weight(LEVELS + l, roll(jnp.where(tail, roll(weight_s[0], place), weight), 1))
        for f in range(4):
            q, k = masked[f], f // 2
            place = 124 - 8 * ((f % 2) * 8 + l)
            h = roll(halo[k], place)
            after = roll(jnp.where(head, h, q), -1)
            edge = edge_sum(roll(jnp.where(tail, h, q), 1), q, after, roll(jnp.where(heads, h, q), -2))
            h = roll(edge_halo[k], place)
            flux = flux_of(
                coefs,
                q,
                after,
                edge,
                roll(jnp.where(tail, h, edge), 1),
                roll(jnp.where(head, h, edge), -1),
            )
            h = roll(flux_s[k][0], place)
            put(f * LEVELS + l, q + roll(jnp.where(tail, h, flux), 1) - flux)


def field_planes():
    return [(p, p) for p in range(32)] + [(STRIP, AD_STRIP), (STRIP + 1, AD_STRIP + 1)]


def y_edges(stack, edges, r):
    for p, to in field_planes():
        edges[to, pl.ds(r, TILE), :] = edge_sum(
            stack[p, pl.ds(r - 1, TILE), :],
            stack[p, pl.ds(r, TILE), :],
            stack[p, pl.ds(r + 1, TILE), :],
            stack[p, pl.ds(r + 2, TILE), :],
        )


def y_fluxes(stack, edges, fluxes, advected, r):
    here, after = pl.ds(r, TILE), pl.ds(r + 1, TILE)

    def put(coefs, p, to):
        fluxes[to, here, :] = flux_of(
            coefs,
            stack[p, here, :],
            stack[p, after, :],
            edges[to, here, :],
            edges[to, pl.ds(r - 1, TILE), :],
            edges[to, after, :],
        )

    shallow = jnp.minimum(stack[DEPTH, here, :], stack[DEPTH, after, :])
    mean_metric = 0.5 * (stack[METRIC, here, :] + stack[METRIC, after, :])
    for l in range(LEVELS):
        opening = shallow > float(l)
        coefs = face_coefs(jnp.where(opening, 0.5 * (stack[VM + l, here, :] + stack[VM + l, after, :]), 0.0))
        advected[WY + l, here, :] = jnp.where(opening, mean_metric, 0.0)
        for f in range(4):
            put(coefs, f * LEVELS + l, f * LEVELS + l)
    level = ((iota(1) >> 3) & 7).astype(F32)
    opening = jnp.minimum(stack[DEPTH_S, here, :], stack[DEPTH_S, after, :]) > level
    coefs = face_coefs(jnp.where(opening, 0.5 * (stack[VM_S, here, :] + stack[VM_S, after, :]), 0.0))
    for k in range(2):
        put(coefs, STRIP + k, AD_STRIP + k)


def y_updates(stack, fluxes, advected, r):
    here, before = pl.ds(r, TILE), pl.ds(r - 1, TILE)
    for p, to in field_planes():
        advected[to, here, :] = stack[p, here, :] + fluxes[to, before, :] - fluxes[to, here, :]


def finish(advected, r, depth, weights, coupling, spreading, put):
    lane = iota(1)
    head, tail = lane == 0, lane == LANES - 1
    here, before, after = pl.ds(r, TILE), pl.ds(r - 1, TILE), pl.ds(r + 1, TILE)
    links, factors, inverses = [], [], []
    for l in range(LEVELS):
        divisor = jnp.ones((TILE, LANES), F32)
        if l < LEVELS - 1:
            links.append(jnp.where(depth > float(l + 1), coupling(l), 0.0))
            divisor = divisor + links[l]
        if l > 0:
            divisor = divisor + links[l - 1] - links[l - 1] * factors[l - 1]
        inverses.append(1.0 / divisor)
        if l < LEVELS - 1:
            factors.append(links[l] * inverses[l])
    for f in range(4):
        reduced = []
        for l in range(LEVELS):
            p = f * LEVELS + l
            a = advected[p, here, :]
            h = roll(advected[AD_STRIP + f // 2, here, :], 124 - 8 * ((f % 2) * 8 + l))
            bend = (
                weights(l) * (roll(jnp.where(head, h, a), -1) - a)
                - weights(LEVELS + l) * (a - roll(jnp.where(tail, h, a), 1))
                + advected[WY + l, here, :] * (advected[p, after, :] - a)
                - advected[WY + l, before, :] * (a - advected[p, before, :])
            )
            target = a + spreading[f, l] * bend
            if l > 0:
                target = target + links[l - 1] * reduced[l - 1]
            reduced.append(target * inverses[l])
        solved = reduced[LEVELS - 1]
        put(f * LEVELS + LEVELS - 1, jnp.where(depth > float(LEVELS - 1), solved, 0.0))
        for l in range(LEVELS - 2, -1, -1):
            solved = reduced[l] + factors[l] * solved
            put(f * LEVELS + l, jnp.where(depth > float(l), solved, 0.0))


def swap_lanes(x, stages):
    lane = iota(1)
    for bit in stages:
        x = jnp.where((lane & bit) != 0, roll(x, bit), roll(x, -bit))
    return x


def edge_kernel(
    lat_ref, t_ref, s_ref, u_ref, v_ref, w_ref, mx_ref, my_ref, own_ref, ownx_ref, fromw_ref, frome_ref,
    a_ref, b_ref, edge_ref,
):
    fields = (t_ref, s_ref, u_ref, v_ref)
    rows_total = mx_ref.shape[0]
    for e, t in enumerate((0, rows_total // TILE - 1)):

        def put(p, x, e=e):
            edge_ref[e, p] = x

        x_tile(t, fields, w_ref, mx_ref, my_ref, own_ref, ownx_ref, fromw_ref, frome_ref, put, None)
    sub = iota(0)
    upper = sub < 4
    lat = lat_ref[0]
    even = (lat & 1) == 0
    fold = lat == lat_ref[1] - 1
    negative = set(range(16, 32)) | set(range(VM, VM + LEVELS)) | {STRIP + 1, VM_S}
    for k in range(PAIRS):
        one, two = 2 * k, min(2 * k + 1, PLANES - 1)
        bottom = jnp.where(upper, edge_ref[0, one], turn(edge_ref[0, two], 4))
        top = jnp.where(upper, turn(edge_ref[1, one], 4), edge_ref[1, two])
        mirror = jnp.where((sub & 1) != 0, turn(top, 1), turn(top, -1))
        mirror = jnp.where((sub & 2) != 0, turn(mirror, 2), turn(mirror, -2))
        mirror = swap_lanes(mirror, (1, 2, 4) if one >= STRIP else (1, 2, 4, 8, 16, 32, 64))
        signs = (-1.0 if one in negative else 1.0, -1.0 if two in negative else 1.0)
        if signs[0] == signs[1]:
            mirror = mirror * signs[0]
        else:
            mirror = mirror * jnp.where(upper, signs[0], signs[1])
        a_ref[k] = jnp.where(even, top, bottom)
        b_ref[k] = jnp.where(even, bottom, jnp.where(fold, mirror, top))


def interior_kernel(
    coef_ref, t_ref, s_ref, u_ref, v_ref, w_ref, mx_ref, my_ref, idf_ref, own_ref, ownx_ref, fromw_ref, frome_ref,
    o0, o1, o2, o3, adv_ref, weight_ref,
    stack, edges, fluxes, advected, weights, out, sems,
):
    fields = (t_ref, s_ref, u_ref, v_ref)
    outs = (o0, o1, o2, o3)
    rows_total = mx_ref.shape[0]
    tiles = rows_total // TILE

    def sweep_x(t, carry):
        start = pl.multiple_of(t * TILE, TILE)

        def put(p, x):
            stack[p, pl.ds(start + TILE, TILE), :] = x

        def put_weight(p, x):
            weights[p, pl.ds(start, TILE), :] = x

        x_tile(t, fields, w_ref, mx_ref, my_ref, own_ref, ownx_ref, fromw_ref, frome_ref, put, put_weight)
        return carry

    def sweep_edges(t, carry):
        y_edges(stack, edges, pl.multiple_of(t * TILE + TILE, TILE))
        return carry

    def sweep_y(t, carry):
        r = pl.multiple_of(t * TILE + TILE, TILE)
        y_fluxes(stack, edges, fluxes, advected, r)
        y_updates(stack, fluxes, advected, r)
        return carry

    def copies(t_rows):
        return [
            pltpu.make_async_copy(out.at[pl.ds(f * LEVELS, LEVELS), t_rows, :], outs[f].at[:, t_rows, :], sems.at[f])
            for f in range(4)
        ]

    def sweep_out(t, carry):
        start = pl.multiple_of(t * TILE, TILE)
        rows = pl.ds(start, TILE)
        depth = stack[DEPTH, pl.ds(start + TILE, TILE), :]

        def put(p, x):
            out[p, rows, :] = x

        finish(
            advected, pl.multiple_of(start + TILE, TILE), depth,
            lambda p: weights[p, rows, :], lambda l: idf_ref[l, rows, :], coef_ref, put,
        )
        for copy in copies(rows):
            copy.start()
        return carry

    lax.fori_loop(0, tiles, sweep_x, 0)
    lax.fori_loop(0, tiles, sweep_edges, 0)
    lax.fori_loop(0, tiles, sweep_y, 0)
    lax.fori_loop(1, tiles - 1, sweep_out, 0)
    for e, start in enumerate((0, rows_total - 2 * TILE)):
        adv_ref[:, pl.ds(e * 2 * TILE, 2 * TILE), :] = advected[:, pl.ds(start + TILE, 2 * TILE), :]
    for e, start in enumerate((0, rows_total - TILE)):
        weight_ref[e] = weights[:, pl.ds(start, TILE), :]
    for copy in copies(pl.ds(TILE, rows_total - 2 * TILE)):
        copy.wait()


def border_kernel(
    lat_ref, coef_ref, idf_lo, idf_hi, a_ref, b_ref, edge_ref, adv_ref, weight_ref, i0, i1, i2, i3,
    o0, o1, o2, o3,
    stack, edges, fluxes, advected, out, sems,
):
    outs = (o0, o1, o2, o3)
    rows_total = o0.shape[1]
    even = (lat_ref[0] & 1) == 0
    started = []
    for e in range(2):
        for p in range(PLANES):
            k = p // 2
            if e == 0:
                halo = jnp.where(even, b_ref[k], a_ref[k])
                stack[p, pl.ds(0, TILE), :] = turn(halo, 4) if p % 2 == 0 else halo
            else:
                halo = jnp.where(even, a_ref[k], b_ref[k])
                stack[p, pl.ds(2 * TILE, TILE), :] = halo if p % 2 == 0 else turn(halo, 4)
            stack[p, pl.ds(TILE, TILE), :] = edge_ref[e, p]
        advected[:, pl.ds(TILE if e == 0 else 0, 2 * TILE), :] = adv_ref[:, pl.ds(e * 2 * TILE, 2 * TILE), :]
        y_edges(stack, edges, 5 if e == 0 else 11)
        y_fluxes(stack, edges, fluxes, advected, 6 if e == 0 else 12)
        y_updates(stack, fluxes, advected, 3 if e == 0 else 13)

        def put(p, x, e=e):
            out[e, p] = x

        idf = idf_lo if e == 0 else idf_hi
        finish(
            advected, TILE, stack[DEPTH, pl.ds(TILE, TILE), :],
            lambda p, e=e: weight_ref[e, p], lambda l, idf=idf: idf[l], coef_ref, put,
        )
        rows = pl.ds(0 if e == 0 else rows_total - TILE, TILE)
        for f in range(4):
            copy = pltpu.make_async_copy(
                out.at[e, pl.ds(f * LEVELS, LEVELS)], outs[f].at[:, rows, :], sems.at[e, f]
            )
            copy.start()
            started.append(copy)
    for copy in started:
        copy.wait()


def vmem(n):
    return [pl.BlockSpec(memory_space=pltpu.VMEM)] * n


def anywhere(n):
    return [pl.BlockSpec(memory_space=pl.ANY)] * n


def smem(n):
    return [pl.BlockSpec(memory_space=pltpu.SMEM)] * n


def shape(*dims):
    return jax.ShapeDtypeStruct(dims, F32)


PARAMS = pltpu.CompilerParams(vmem_limit_bytes=40 * 1024 * 1024)


def shards(heat, salt, east, north, water, metric_x, metric_y, diffusion, spreading, mirror):
    rows, cols = metric_x.shape
    lon_count, lat_count = lax.axis_size("lon"), lax.axis_size("lat")
    lon, lat = lax.axis_index("lon"), lax.axis_index("lat")
    lat_info = jnp.stack([lat, jnp.int32(lat_count)]).astype(jnp.int32)
    pivot = (mirror[0] // cols + lon) % lon_count

    base = (heat, salt, east, north, water, metric_x, metric_y)
    own, ownx, to_east, to_west = pl.pallas_call(
        pack_kernel,
        out_shape=(shape(2, rows, LANES), shape(3, TILE, LANES), shape(rows + 16, LANES), shape(rows + 16, LANES)),
        in_specs=vmem(7),
        out_specs=tuple(vmem(4)),
        compiler_params=PARAMS,
    )(*base)
    ring = [(i, (i + 1) % lon_count) for i in range(lon_count)]
    from_west = lax.ppermute(to_east, "lon", ring)
    from_east = lax.ppermute(to_west, "lon", [(j, i) for i, j in ring])
    sides = (own, ownx, from_west, from_east)

    rows_a, rows_b, edge = pl.pallas_call(
        edge_kernel,
        out_shape=(shape(PAIRS, TILE, LANES), shape(PAIRS, TILE, LANES), shape(2, PLANES, TILE, LANES)),
        in_specs=smem(1) + vmem(11),
        out_specs=tuple(vmem(3)),
        compiler_params=PARAMS,
    )(lat_info, *base, *sides)

    index = lambda o, a: o * lat_count + a
    pairs = [(index(o, a), index(o, a ^ 1)) for o in range(lon_count) for a in range(lat_count)]
    got_a = lax.ppermute(rows_a, ("lon", "lat"), pairs)

    def across(k, x):
        fixed = []
        for o in range(lon_count):
            for a in range(1, lat_count - 1):
                fixed.append((index(o, a), index(o, ((a + 1) ^ 1) - 1)))
            fixed.append((index(o, lat_count - 1), index((k - o) % lon_count, lat_count - 1)))
        return lax.ppermute(x, ("lon", "lat"), fixed)

    got_b = lax.switch(pivot, [functools.partial(across, k) for k in range(lon_count)], rows_b)

    stack_rows = rows + 2 * TILE
    results = pl.pallas_call(
        interior_kernel,
        out_shape=(shape(LEVELS, rows, cols),) * 4 + (shape(AD_PLANES, 4 * TILE, LANES), shape(2, 16, TILE, LANES)),
        in_specs=smem(1) + vmem(12),
        out_specs=tuple(anywhere(4) + vmem(2)),
        scratch_shapes=[
            pltpu.VMEM((PLANES, stack_rows, LANES), F32),
            pltpu.VMEM((34, stack_rows, LANES), F32),
            pltpu.VMEM((34, stack_rows, LANES), F32),
            pltpu.VMEM((AD_PLANES, stack_rows, LANES), F32),
            pltpu.VMEM((16, rows, LANES), F32),
            pltpu.VMEM((32, rows, LANES), F32),
            pltpu.SemaphoreType.DMA((4,)),
        ],
        compiler_params=PARAMS,
    )(spreading, *base, diffusion, *sides)
    outs, advected, weights = results[:4], results[4], results[5]

    last = rows // TILE - 1
    return pl.pallas_call(
        border_kernel,
        grid=(1,),
        out_shape=(shape(LEVELS, rows, cols),) * 4,
        in_specs=smem(2)
        + [
            pl.BlockSpec((LEVELS - 1, TILE, cols), lambda i: (0, 0, 0)),
            pl.BlockSpec((LEVELS - 1, TILE, cols), lambda i: (0, last, 0)),
        ]
        + vmem(5)
        + anywhere(4),
        out_specs=tuple(anywhere(4)),
        scratch_shapes=[
            pltpu.VMEM((PLANES, 3 * TILE, LANES), F32),
            pltpu.VMEM((34, 3 * TILE, LANES), F32),
            pltpu.VMEM((34, 3 * TILE, LANES), F32),
            pltpu.VMEM((AD_PLANES, 3 * TILE, LANES), F32),
            pltpu.VMEM((2, 32, TILE, LANES), F32),
            pltpu.SemaphoreType.DMA((2, 4)),
        ],
        input_output_aliases={9 + f: f for f in range(4)},
        compiler_params=PARAMS,
    )(lat_info, spreading, diffusion, diffusion, got_a, got_b, edge, advected, weights, *outs)


def solution(mesh):
    block = P(None, "lat", "lon")
    in_specs = (block,) * 5 + (P("lat", "lon"),) * 2 + (block, P(), P("lon"))
    return jax.shard_map(shards, mesh=mesh, in_specs=in_specs, out_specs=(block,) * 4, check_vma=False)
```

```python
import functools
import jax
import jax.numpy as jnp
from jax import lax
from jax.experimental import pallas as pl
from jax.experimental.pallas import tpu as pltpu
from jax.sharding import PartitionSpec as P

F32 = jnp.float32
LEVELS = 8
TILE = 8
LANES = 128
VM, DEPTH, METRIC, STRIP, VM_S, DEPTH_S, METRIC_S, PLANES = 32, 40, 41, 42, 44, 45, 46, 47
PAIRS = 24
AD_STRIP, WY, AD_PLANES = 32, 34, 42


def roll(x, shift):
    shift %= LANES
    return x if shift == 0 else pltpu.roll(x, shift, 1)


def turn(x, shift):
    return pltpu.roll(x, shift % TILE, 0)


def iota(dimension):
    return lax.broadcasted_iota(jnp.int32, (TILE, LANES), dimension)


def face_coefs(courant):
    size = jnp.abs(courant)
    rest = 1.0 - size
    edge = courant * rest * (1.0 / 12.0)
    return edge * rest, courant * size * (3.0 - 2.0 * size), edge * size, courant >= 0.0


def edge_sum(before, here, after, beyond):
    return 7.0 * (here + after) - (before + beyond)


def flux_of(coefs, here, after, edge, edge_before, edge_after):
    own, centre, far, positive = coefs
    return own * edge + centre * jnp.where(positive, here, after) - far * jnp.where(positive, edge_before, edge_after)


def pack_kernel(t_ref, s_ref, u_ref, v_ref, w_ref, mx_ref, my_ref, own_ref, ownx_ref, toe_ref, tow_ref):
    fields = (t_ref, s_ref, u_ref, v_ref)
    step, tiles = pl.program_id(0), mx_ref.shape[0] // TILE
    rows_total = toe_ref.shape[0] - 2 * TILE
    lane = iota(1)
    low = (lane & 7) < 4
    group = lane >> 3
    zero = jnp.zeros((TILE, LANES), F32)

    @pl.when(step == 0)
    def _():
        for i in range(3):
            ownx_ref[i] = zero

    def body(t, carry):
        rows = pl.ds(pl.multiple_of(t * TILE, TILE), TILE)
        tile = t + step * tiles
        whole = pl.ds(pl.multiple_of(tile * TILE, TILE), TILE)
        wet = [w_ref[l, rows, :] for l in range(LEVELS)]
        depth = sum(wet[1:], wet[0]).astype(F32)
        packs = []
        for k in range(2):
            pack = zero
            for p in range(16):
                q = jnp.where(wet[p % 8] != 0, fields[2 * k + p // 8][p % 8, rows, :], 0.0)
                pack = jnp.where(group == p, roll(q, 4 + 8 * p), pack)
            packs.append(pack)
            own_ref[k, rows, :] = pack
        toe_ref[whole, :] = jnp.where(low, packs[0], roll(packs[1], 4))
        tow_ref[whole, :] = jnp.where(low, roll(packs[1], -4), packs[0])
        shift = (4 + 8 * tile) & (LANES - 1)
        for i, x in enumerate((depth, mx_ref[rows, :], my_ref[rows, :])):
            ownx_ref[i] = jnp.where(group == tile, pltpu.roll(x, shift, 1), ownx_ref[i])
        return carry

    lax.fori_loop(0, tiles, body, 0)

    @pl.when(step == pl.num_programs(0) - 1)
    def _():
        depth, metric_x, metric_y = ownx_ref[0], ownx_ref[1], ownx_ref[2]
        first, second = pl.ds(rows_total, TILE), pl.ds(rows_total + TILE, TILE)
        toe_ref[first, :] = jnp.where(low, depth, roll(metric_x, 4))
        toe_ref[second, :] = jnp.where(low, metric_y, 0.0)
        tow_ref[first, :] = jnp.where(low, roll(metric_x, -4), depth)
        tow_ref[second, :] = jnp.where(low, 0.0, metric_y)


def x_tile(t, fields, w_ref, mx_ref, my_ref, own_ref, ownx_ref, fromw_ref, frome_ref, put, put_weight):
    rows_total = mx_ref.shape[0]
    start = pl.multiple_of(t * TILE, TILE)
    rows = pl.ds(start, TILE)
    lane = iota(1)
    low = (lane & 7) < 4
    group = lane >> 3
    level = (group & 7).astype(F32)
    half = lane < 64
    west, east = fromw_ref[rows, :], frome_ref[rows, :]
    halo = (jnp.where(low, west, east), jnp.where(low, roll(west, -4), roll(east, 4)))
    own = (own_ref[0, rows, :], own_ref[1, rows, :])
    strips = [(jnp.where(low, halo[k], own[k]), jnp.where(low, own[k], halo[k])) for k in range(2)]
    first, second = pl.ds(rows_total, TILE), pl.ds(rows_total + TILE, TILE)
    west, east = fromw_ref[first, :], frome_ref[first, :]
    west_2, east_2 = fromw_ref[second, :], frome_ref[second, :]
    side_halo = (
        jnp.where(low, west, east),
        jnp.where(low, roll(west, -4), roll(east, 4)),
        jnp.where(low, west_2, east_2),
    )

    def spread(x):
        x = jnp.where(group == t, x, 0.0)
        for shift in (8, 16, 32, 64):
            x = x + roll(x, shift)
        return x

    extra = []
    for i in range(3):
        mine = ownx_ref[i]
        extra.append((spread(jnp.where(low, side_halo[i], mine)), spread(jnp.where(low, mine, side_halo[i]))))
    depth_s, mx_s, my_s = extra

    um_s, weight_s, edge_s, flux_s, star_s, vm_s = [], [], [[], []], [[], []], [[], []], []
    for side in range(2):
        mixed = strips[1][side]
        swapped = roll(mixed, 64)
        um = jnp.where(half, mixed, swapped) * mx_s[side]
        vm_s.append(jnp.where(half, swapped, mixed) * my_s[side])
        opening = jnp.minimum(depth_s[side], roll(depth_s[side], -1)) > level
        coefs = face_coefs(jnp.where(opening, 0.5 * (um + roll(um, -1)), 0.0))
        um_s.append(um)
        weight_s.append(jnp.where(opening, 0.5 * (mx_s[side] + roll(mx_s[side], -1)), 0.0))
        for k in range(2):
            q = strips[k][side]
            after = roll(q, -1)
            edge = edge_sum(roll(q, 1), q, after, roll(q, -2))
            flux = flux_of(coefs, q, after, edge, roll(edge, 1), roll(edge, -1))
            edge_s[k].append(edge)
            flux_s[k].append(flux)
            star_s[k].append(q + roll(flux, 1) - flux)
    um_halo = jnp.where(low, um_s[0], um_s[1])
    edge_halo = [jnp.where(low, edge_s[k][0], edge_s[k][1]) for k in range(2)]
    for k in range(2):
        put(STRIP + k, jnp.where(low, star_s[k][0], star_s[k][1]))
    put(VM_S, jnp.where(low, vm_s[0], vm_s[1]))
    put(DEPTH_S, jnp.where(low, depth_s[0], depth_s[1]))
    put(METRIC_S, jnp.where(low, my_s[0], my_s[1]))

    head, tail, heads = lane == 0, lane == LANES - 1, lane < 2
    wet = [w_ref[l, rows, :] for l in range(LEVELS)]
    depth = sum(wet[1:], wet[0]).astype(F32)
    mx, my = mx_ref[rows, :], my_ref[rows, :]
    put(DEPTH, depth)
    put(METRIC, my)
    shallow = jnp.minimum(depth, roll(jnp.where(head, roll(depth_s[1], -4), depth), -1))
    mean_metric = 0.5 * (mx + roll(jnp.where(head, roll(mx_s[1], -4), mx), -1))
    for l in range(LEVELS):
        masked = [jnp.where(wet[l] != 0, field[l, rows, :], 0.0) for field in fields]
        um = masked[2] * mx
        put(VM + l, masked[3] * my)
        opening = shallow > float(l)
        place = 124 - 8 * l
        coefs = face_coefs(
            jnp.where(opening, 0.5 * (um + roll(jnp.where(head, roll(um_halo, place), um), -1)), 0.0)
        )
        if put_weight is not None:
            weight = jnp.where(opening, mean_metric, 0.0)
            put_weight(l, weight)
            put_weight(LEVELS + l, roll(jnp.where(tail, roll(weight_s[0], place), weight), 1))
        for f in range(4):
            q, k = masked[f], f // 2
            place = 124 - 8 * ((f % 2) * 8 + l)
            h = roll(halo[k], place)
            after = roll(jnp.where(head, h, q), -1)
            edge = edge_sum(roll(jnp.where(tail, h, q), 1), q, after, roll(jnp.where(heads, h, q), -2))
            h = roll(edge_halo[k], place)
            flux = flux_of(
                coefs,
                q,
                after,
                edge,
                roll(jnp.where(tail, h, edge), 1),
                roll(jnp.where(head, h, edge), -1),
            )
            h = roll(flux_s[k][0], place)
            put(f * LEVELS + l, q + roll(jnp.where(tail, h, flux), 1) - flux)


def field_planes():
    return [(p, p) for p in range(32)] + [(STRIP, AD_STRIP), (STRIP + 1, AD_STRIP + 1)]


def y_edges(stack, edges, r):
    for p, to in field_planes():
        edges[to, pl.ds(r, TILE), :] = edge_sum(
            stack[p, pl.ds(r - 1, TILE), :],
            stack[p, pl.ds(r, TILE), :],
            stack[p, pl.ds(r + 1, TILE), :],
            stack[p, pl.ds(r + 2, TILE), :],
        )


def y_fluxes(stack, edges, fluxes, advected, r):
    here, after = pl.ds(r, TILE), pl.ds(r + 1, TILE)

    def put(coefs, p, to):
        fluxes[to, here, :] = flux_of(
            coefs,
            stack[p, here, :],
            stack[p, after, :],
            edges[to, here, :],
            edges[to, pl.ds(r - 1, TILE), :],
            edges[to, after, :],
        )

    shallow = jnp.minimum(stack[DEPTH, here, :], stack[DEPTH, after, :])
    mean_metric = 0.5 * (stack[METRIC, here, :] + stack[METRIC, after, :])
    for l in range(LEVELS):
        opening = shallow > float(l)
        coefs = face_coefs(jnp.where(opening, 0.5 * (stack[VM + l, here, :] + stack[VM + l, after, :]), 0.0))
        advected[WY + l, here, :] = jnp.where(opening, mean_metric, 0.0)
        for f in range(4):
            put(coefs, f * LEVELS + l, f * LEVELS + l)
    level = ((iota(1) >> 3) & 7).astype(F32)
    opening = jnp.minimum(stack[DEPTH_S, here, :], stack[DEPTH_S, after, :]) > level
    coefs = face_coefs(jnp.where(opening, 0.5 * (stack[VM_S, here, :] + stack[VM_S, after, :]), 0.0))
    for k in range(2):
        put(coefs, STRIP + k, AD_STRIP + k)


def y_updates(stack, fluxes, advected, r):
    here, before = pl.ds(r, TILE), pl.ds(r - 1, TILE)
    for p, to in field_planes():
        advected[to, here, :] = stack[p, here, :] + fluxes[to, before, :] - fluxes[to, here, :]


def finish(advected, r, depth, weights, coupling, spreading, put):
    lane = iota(1)
    head, tail = lane == 0, lane == LANES - 1
    here, before, after = pl.ds(r, TILE), pl.ds(r - 1, TILE), pl.ds(r + 1, TILE)
    links, factors, inverses = [], [], []
    for l in range(LEVELS):
        divisor = jnp.ones((TILE, LANES), F32)
        if l < LEVELS - 1:
            links.append(jnp.where(depth > float(l + 1), coupling(l), 0.0))
            divisor = divisor + links[l]
        if l > 0:
            divisor = divisor + links[l - 1] - links[l - 1] * factors[l - 1]
        inverses.append(1.0 / divisor)
        if l < LEVELS - 1:
            factors.append(links[l] * inverses[l])
    for f in range(4):
        reduced = []
        for l in range(LEVELS):
            p = f * LEVELS + l
            a = advected[p, here, :]
            h = roll(advected[AD_STRIP + f // 2, here, :], 124 - 8 * ((f % 2) * 8 + l))
            bend = (
                weights(l) * (roll(jnp.where(head, h, a), -1) - a)
                - weights(LEVELS + l) * (a - roll(jnp.where(tail, h, a), 1))
                + advected[WY + l, here, :] * (advected[p, after, :] - a)
                - advected[WY + l, before, :] * (a - advected[p, before, :])
            )
            target = a + spreading[f, l] * bend
            if l > 0:
                target = target + links[l - 1] * reduced[l - 1]
            reduced.append(target * inverses[l])
        solved = reduced[LEVELS - 1]
        put(f * LEVELS + LEVELS - 1, jnp.where(depth > float(LEVELS - 1), solved, 0.0))
        for l in range(LEVELS - 2, -1, -1):
            solved = reduced[l] + factors[l] * solved
            put(f * LEVELS + l, jnp.where(depth > float(l), solved, 0.0))


def edge_kernel(
    lat_ref, t_ref, s_ref, u_ref, v_ref, w_ref, mx_ref, my_ref, own_ref, ownx_ref, fromw_ref, frome_ref,
    a_ref, b_ref, edge_ref,
):
    fields = (t_ref, s_ref, u_ref, v_ref)
    tiles = mx_ref.shape[0] // TILE

    def sweep(e, carry):
        def put(p, x):
            edge_ref[e, p] = x

        x_tile(e * (tiles - 1), fields, w_ref, mx_ref, my_ref, own_ref, ownx_ref, fromw_ref, frome_ref, put, None)
        return carry

    lax.fori_loop(0, 2, sweep, 0)
    lane, sub = iota(1), iota(0)
    upper = sub < 4
    lat = lat_ref[0]
    even = (lat & 1) == 0
    fold = lat == lat_ref[1] - 1

    def send(k, lanes, first_sign, second_sign):
        one, two = 2 * k, 2 * k + 1
        bottom = jnp.where(upper, edge_ref[0, one], turn(edge_ref[0, two], 4))
        top = jnp.where(upper, turn(edge_ref[1, one], 4), edge_ref[1, two])
        mirror = jnp.where((sub & 1) != 0, turn(top, 1), turn(top, -1))
        mirror = jnp.where((sub & 2) != 0, turn(mirror, 2), turn(mirror, -2))
        mirror = jnp.take_along_axis(mirror, lanes, axis=1) * jnp.where(upper, first_sign, second_sign)
        a_ref[k] = jnp.where(even, top, bottom)
        b_ref[k] = jnp.where(even, bottom, jnp.where(fold, mirror, top))

    def send_plain(i, carry):
        for k in range(3):
            pair = i * 3 + k
            sign = jnp.where((pair >= 8) & (pair < 20), -1.0, 1.0)
            send(pair, LANES - 1 - lane, sign, sign)
        return carry

    lax.fori_loop(0, STRIP // 6, send_plain, 0)
    for e in range(2):
        edge_ref[e, PLANES] = jnp.zeros((TILE, LANES), F32)
    send(STRIP // 2, lane ^ 7, 1.0, -1.0)
    send(STRIP // 2 + 1, lane ^ 7, -1.0, 1.0)
    send(STRIP // 2 + 2, lane ^ 7, 1.0, 1.0)


def interior_kernel(
    coef_ref, t_ref, s_ref, u_ref, v_ref, w_ref, mx_ref, my_ref, idf_ref, own_ref, ownx_ref, fromw_ref, frome_ref,
    o0, o1, o2, o3, adv_ref, weight_ref,
    stack, edges, fluxes, advected, weights, out, sems,
):
    fields = (t_ref, s_ref, u_ref, v_ref)
    outs = (o0, o1, o2, o3)
    rows_total = mx_ref.shape[0]
    tiles = rows_total // TILE

    def sweep_x(t, carry):
        start = pl.multiple_of(t * TILE, TILE)

        def put(p, x):
            stack[p, pl.ds(start + TILE, TILE), :] = x

        def put_weight(p, x):
            weights[p, pl.ds(start, TILE), :] = x

        x_tile(t, fields, w_ref, mx_ref, my_ref, own_ref, ownx_ref, fromw_ref, frome_ref, put, put_weight)
        return carry

    def sweep_edges(t, carry):
        y_edges(stack, edges, pl.multiple_of(t * TILE + TILE, TILE))
        return carry

    def sweep_y(t, carry):
        r = pl.multiple_of(t * TILE + TILE, TILE)
        y_fluxes(stack, edges, fluxes, advected, r)
        y_updates(stack, fluxes, advected, r)
        return carry

    def copies(t_rows):
        return [
            pltpu.make_async_copy(out.at[pl.ds(f * LEVELS, LEVELS), t_rows, :], outs[f].at[:, t_rows, :], sems.at[f])
            for f in range(4)
        ]

    def sweep_out(t, carry):
        start = pl.multiple_of(t * TILE, TILE)
        rows = pl.ds(start, TILE)
        depth = stack[DEPTH, pl.ds(start + TILE, TILE), :]

        def put(p, x):
            out[p, rows, :] = x

        finish(
            advected, pl.multiple_of(start + TILE, TILE), depth,
            lambda p: weights[p, rows, :], lambda l: idf_ref[l, rows, :], coef_ref, put,
        )
        for copy in copies(rows):
            copy.start()
        return carry

    lax.fori_loop(0, tiles, sweep_x, 0)
    lax.fori_loop(0, tiles, sweep_edges, 0)
    lax.fori_loop(0, tiles, sweep_y, 0)
    lax.fori_loop(1, tiles - 1, sweep_out, 0)
    for e, start in enumerate((0, rows_total - 2 * TILE)):
        adv_ref[:, pl.ds(e * 2 * TILE, 2 * TILE), :] = advected[:, pl.ds(start + TILE, 2 * TILE), :]
    for e, start in enumerate((0, rows_total - TILE)):
        weight_ref[e] = weights[:, pl.ds(start, TILE), :]
    for copy in copies(pl.ds(TILE, rows_total - 2 * TILE)):
        copy.wait()


def border_kernel(
    lat_ref, coef_ref, idf_lo, idf_hi, a_ref, b_ref, edge_ref, adv_ref, weight_ref, i0, i1, i2, i3,
    o0, o1, o2, o3,
    stack, edges, fluxes, advected, out, sems,
):
    outs = (o0, o1, o2, o3)
    rows_total = o0.shape[1]
    even = (lat_ref[0] & 1) == 0
    started = []
    for e in range(2):
        for p in range(PLANES):
            k = p // 2
            if e == 0:
                halo = jnp.where(even, b_ref[k], a_ref[k])
                stack[p, pl.ds(0, TILE), :] = turn(halo, 4) if p % 2 == 0 else halo
            else:
                halo = jnp.where(even, a_ref[k], b_ref[k])
                stack[p, pl.ds(2 * TILE, TILE), :] = halo if p % 2 == 0 else turn(halo, 4)
            stack[p, pl.ds(TILE, TILE), :] = edge_ref[e, p]
        advected[:, pl.ds(TILE if e == 0 else 0, 2 * TILE), :] = adv_ref[:, pl.ds(e * 2 * TILE, 2 * TILE), :]
        y_edges(stack, edges, 5 if e == 0 else 11)
        y_fluxes(stack, edges, fluxes, advected, 6 if e == 0 else 12)
        y_updates(stack, fluxes, advected, 3 if e == 0 else 13)

        def put(p, x, e=e):
            out[e, p] = x

        idf = idf_lo if e == 0 else idf_hi
        finish(
            advected, TILE, stack[DEPTH, pl.ds(TILE, TILE), :],
            lambda p, e=e: weight_ref[e, p], lambda l, idf=idf: idf[l], coef_ref, put,
        )
        rows = pl.ds(0 if e == 0 else rows_total - TILE, TILE)
        for f in range(4):
            copy = pltpu.make_async_copy(
                out.at[e, pl.ds(f * LEVELS, LEVELS)], outs[f].at[:, rows, :], sems.at[e, f]
            )
            copy.start()
            started.append(copy)
    for copy in started:
        copy.wait()


def vmem(n):
    return [pl.BlockSpec(memory_space=pltpu.VMEM)] * n


def anywhere(n):
    return [pl.BlockSpec(memory_space=pl.ANY)] * n


def smem(n):
    return [pl.BlockSpec(memory_space=pltpu.SMEM)] * n


def shape(*dims):
    return jax.ShapeDtypeStruct(dims, F32)


PARAMS = pltpu.CompilerParams(vmem_limit_bytes=40 * 1024 * 1024)


def call_pack(base):
    rows, cols = base[5].shape
    steps = 2
    part = rows // steps
    wide = lambda: pl.BlockSpec((LEVELS, part, cols), lambda i: (0, i, 0))
    flat = lambda: pl.BlockSpec((part, cols), lambda i: (i, 0))
    return pl.pallas_call(
        pack_kernel,
        grid=(steps,),
        out_shape=(shape(2, rows, LANES), shape(3, TILE, LANES), shape(rows + 16, LANES), shape(rows + 16, LANES)),
        in_specs=[wide() for _ in range(5)] + [flat(), flat()],
        out_specs=(
            pl.BlockSpec((2, part, LANES), lambda i: (0, i, 0)),
            pl.BlockSpec((3, TILE, LANES), lambda i: (0, 0, 0)),
            pl.BlockSpec((rows + 16, LANES), lambda i: (0, 0)),
            pl.BlockSpec((rows + 16, LANES), lambda i: (0, 0)),
        ),
    )(*base)


def call_edge(lat_info, base, sides):
    return pl.pallas_call(
        edge_kernel,
        out_shape=(shape(PAIRS, TILE, LANES), shape(PAIRS, TILE, LANES), shape(2, 2 * PAIRS, TILE, LANES)),
        in_specs=smem(1) + vmem(11),
        out_specs=tuple(vmem(3)),
        compiler_params=PARAMS,
    )(lat_info, *base, *sides)


def call_interior(spreading, base, diffusion, sides):
    rows, cols = base[5].shape
    stack_rows = rows + 2 * TILE
    return pl.pallas_call(
        interior_kernel,
        out_shape=(shape(LEVELS, rows, cols),) * 4 + (shape(AD_PLANES, 4 * TILE, LANES), shape(2, 16, TILE, LANES)),
        in_specs=smem(1) + vmem(12),
        out_specs=tuple(anywhere(4) + vmem(2)),
        scratch_shapes=[
            pltpu.VMEM((PLANES, stack_rows, LANES), F32),
            pltpu.VMEM((34, stack_rows, LANES), F32),
            pltpu.VMEM((34, stack_rows, LANES), F32),
            pltpu.VMEM((AD_PLANES, stack_rows, LANES), F32),
            pltpu.VMEM((16, rows, LANES), F32),
            pltpu.VMEM((32, rows, LANES), F32),
            pltpu.SemaphoreType.DMA((4,)),
        ],
        compiler_params=PARAMS,
    )(spreading, *base, diffusion, *sides)


def call_border(lat_info, spreading, diffusion, got_a, got_b, edge, advected, weights, outs):
    _, rows, cols = outs[0].shape
    last = rows // TILE - 1
    return pl.pallas_call(
        border_kernel,
        grid=(1,),
        out_shape=(shape(LEVELS, rows, cols),) * 4,
        in_specs=smem(2)
        + [
            pl.BlockSpec((LEVELS - 1, TILE, cols), lambda i: (0, 0, 0)),
            pl.BlockSpec((LEVELS - 1, TILE, cols), lambda i: (0, last, 0)),
        ]
        + vmem(5)
        + anywhere(4),
        out_specs=tuple(anywhere(4)),
        scratch_shapes=[
            pltpu.VMEM((PLANES, 3 * TILE, LANES), F32),
            pltpu.VMEM((34, 3 * TILE, LANES), F32),
            pltpu.VMEM((34, 3 * TILE, LANES), F32),
            pltpu.VMEM((AD_PLANES, 3 * TILE, LANES), F32),
            pltpu.VMEM((2, 32, TILE, LANES), F32),
            pltpu.SemaphoreType.DMA((2, 4)),
        ],
        input_output_aliases={9 + f: f for f in range(4)},
        compiler_params=PARAMS,
    )(lat_info, spreading, diffusion, diffusion, got_a, got_b, edge, advected, weights, *outs)


def shards(heat, salt, east, north, water, metric_x, metric_y, diffusion, spreading, mirror):
    cols = metric_x.shape[1]
    lon_count, lat_count = lax.axis_size("lon"), lax.axis_size("lat")
    lon, lat = lax.axis_index("lon"), lax.axis_index("lat")
    lat_info = jnp.stack([lat, jnp.int32(lat_count)]).astype(jnp.int32)
    pivot = (mirror[0] // cols + lon) % lon_count

    base = (heat, salt, east, north, water, metric_x, metric_y)
    own, ownx, to_east, to_west = call_pack(base)
    ring = [(i, (i + 1) % lon_count) for i in range(lon_count)]
    from_west = lax.ppermute(to_east, "lon", ring)
    from_east = lax.ppermute(to_west, "lon", [(j, i) for i, j in ring])
    sides = (own, ownx, from_west, from_east)
    rows_a, rows_b, edge = call_edge(lat_info, base, sides)

    index = lambda o, a: o * lat_count + a
    pairs = [(index(o, a), index(o, a ^ 1)) for o in range(lon_count) for a in range(lat_count)]
    got_a = lax.ppermute(rows_a, ("lon", "lat"), pairs)

    def across(k, x):
        fixed = []
        for o in range(lon_count):
            for a in range(1, lat_count - 1):
                fixed.append((index(o, a), index(o, ((a + 1) ^ 1) - 1)))
            fixed.append((index(o, lat_count - 1), index((k - o) % lon_count, lat_count - 1)))
        return lax.ppermute(x, ("lon", "lat"), fixed)

    got_b = lax.switch(pivot, [functools.partial(across, k) for k in range(lon_count)], rows_b)
    results = call_interior(spreading, base, diffusion, sides)
    return call_border(lat_info, spreading, diffusion, got_a, got_b, edge, results[4], results[5], results[:4])


def solution(mesh):
    block = P(None, "lat", "lon")
    in_specs = (block,) * 5 + (P("lat", "lon"),) * 2 + (block, P(), P("lon"))
    return jax.shard_map(shards, mesh=mesh, in_specs=in_specs, out_specs=(block,) * 4, check_vma=False)
```

```python
import functools
import jax
import jax.numpy as jnp
from jax import lax
from jax.experimental import pallas as pl
from jax.experimental.pallas import tpu as pltpu
from jax.sharding import PartitionSpec as P

F32 = jnp.float32
LEVELS = 8
TILE = 8
LANES = 128
VM, DEPTH, METRIC, STRIP, VM_S, DEPTH_S, METRIC_S, PLANES = 32, 40, 41, 42, 44, 45, 46, 47
PAIRS = 24
FACES, TURNED = 37, 44
AD_STRIP, WY, AD_PLANES = 32, 34, 36


def roll(x, shift):
    shift %= LANES
    return x if shift == 0 else pltpu.roll(x, shift, 1)


def turn(x, shift):
    return pltpu.roll(x, shift % TILE, 0)


def iota(dimension):
    return lax.broadcasted_iota(jnp.int32, (TILE, LANES), dimension)


def face_coefs(courant):
    size = jnp.abs(courant)
    rest = 1.0 - size
    edge = courant * rest * (1.0 / 12.0)
    return edge * rest, courant * size * (3.0 - 2.0 * size), edge * size, courant >= 0.0


def edge_sum(before, here, after, beyond):
    return 7.0 * (here + after) - (before + beyond)


def flux_of(coefs, here, after, edge, edge_before, edge_after):
    own, centre, far, positive = coefs
    return own * edge + centre * jnp.where(positive, here, after) - far * jnp.where(positive, edge_before, edge_after)


def pack_kernel(t_ref, s_ref, u_ref, v_ref, w_ref, mx_ref, my_ref, own_ref, ownx_ref, toe_ref, tow_ref, depths):
    fields = (t_ref, s_ref, u_ref, v_ref)
    step, tiles = pl.program_id(0), t_ref.shape[1] // TILE
    rows_total = mx_ref.shape[0]
    lane = iota(1)
    low = (lane & 7) < 4
    group = lane >> 3
    zero = jnp.zeros((TILE, LANES), F32)

    @pl.when(step == 0)
    def _():
        for i in range(3):
            ownx_ref[i] = zero

    def body(t, carry):
        rows = pl.ds(pl.multiple_of(t * TILE, TILE), TILE)
        tile = t + step * tiles
        whole = pl.ds(pl.multiple_of(tile * TILE, TILE), TILE)
        wet = [w_ref[l, rows, :] for l in range(LEVELS)]
        depth = sum(wet[1:], wet[0]).astype(F32)
        packs = []
        for k in range(2):
            pack = zero
            for p in range(16):
                q = jnp.where(wet[p % 8] != 0, fields[2 * k + p // 8][p % 8, rows, :], 0.0)
                pack = jnp.where(group == p, roll(q, 4 + 8 * p), pack)
            packs.append(pack)
            own_ref[k, rows, :] = pack
        toe_ref[whole, :] = jnp.where(low, packs[0], roll(packs[1], 4))
        tow_ref[whole, :] = jnp.where(low, roll(packs[1], -4), packs[0])
        shift = (4 + 8 * tile) & (LANES - 1)
        depths[whole, :] = depth
        for i, x in enumerate((depth, mx_ref[whole, :], my_ref[whole, :])):
            ownx_ref[i] = jnp.where(group == tile, pltpu.roll(x, shift, 1), ownx_ref[i])
        return carry

    lax.fori_loop(0, tiles, body, 0)

    @pl.when(step == pl.num_programs(0) - 1)
    def _():
        depth, metric_x, metric_y = ownx_ref[0], ownx_ref[1], ownx_ref[2]
        first, second = pl.ds(rows_total, TILE), pl.ds(rows_total + TILE, TILE)
        toe_ref[first, :] = jnp.where(low, depth, roll(metric_x, 4))
        toe_ref[second, :] = jnp.where(low, metric_y, 0.0)
        tow_ref[first, :] = jnp.where(low, roll(metric_x, -4), depth)
        tow_ref[second, :] = jnp.where(low, 0.0, metric_y)
        upper = iota(0) < 4
        turned = [x[...].T for x in (depths, mx_ref, my_ref)]
        starts = [x[:TILE] for x in turned]
        ends = [x[-TILE:] for x in turned]
        third, fourth = pl.ds(rows_total + 2 * TILE, TILE), pl.ds(rows_total + 3 * TILE, TILE)
        toe_ref[third, :] = jnp.where(upper, turn(ends[0], 4), ends[1])
        tow_ref[third, :] = jnp.where(upper, starts[1], turn(starts[0], 4))
        toe_ref[fourth, :] = jnp.where(upper, turn(ends[2], 4), 0.0)
        tow_ref[fourth, :] = jnp.where(upper, 0.0, turn(starts[2], 4))


def x_tile(t, fields, w_ref, mx_ref, my_ref, own_ref, ownx_ref, fromw_ref, frome_ref, put):
    rows_total = mx_ref.shape[0]
    start = pl.multiple_of(t * TILE, TILE)
    rows = pl.ds(start, TILE)
    lane = iota(1)
    low = (lane & 7) < 4
    group = lane >> 3
    level = (group & 7).astype(F32)
    half = lane < 64
    west, east = fromw_ref[rows, :], frome_ref[rows, :]
    halo = (jnp.where(low, west, east), jnp.where(low, roll(west, -4), roll(east, 4)))
    own = (own_ref[0, rows, :], own_ref[1, rows, :])
    strips = [(jnp.where(low, halo[k], own[k]), jnp.where(low, own[k], halo[k])) for k in range(2)]
    first, second = pl.ds(rows_total, TILE), pl.ds(rows_total + TILE, TILE)
    west, east = fromw_ref[first, :], frome_ref[first, :]
    west_2, east_2 = fromw_ref[second, :], frome_ref[second, :]
    side_halo = (
        jnp.where(low, west, east),
        jnp.where(low, roll(west, -4), roll(east, 4)),
        jnp.where(low, west_2, east_2),
    )

    def spread(x):
        x = jnp.where(group == t, x, 0.0)
        for shift in (8, 16, 32, 64):
            x = x + roll(x, shift)
        return x

    extra = []
    for i in range(3):
        mine = ownx_ref[i]
        extra.append((spread(jnp.where(low, side_halo[i], mine)), spread(jnp.where(low, mine, side_halo[i]))))
    depth_s, mx_s, my_s = extra

    um_s, edge_s, flux_s, star_s, vm_s = [], [[], []], [[], []], [[], []], []
    for side in range(2):
        mixed = strips[1][side]
        swapped = roll(mixed, 64)
        um = jnp.where(half, mixed, swapped) * mx_s[side]
        vm_s.append(jnp.where(half, swapped, mixed) * my_s[side])
        opening = jnp.minimum(depth_s[side], roll(depth_s[side], -1)) > level
        coefs = face_coefs(jnp.where(opening, 0.5 * (um + roll(um, -1)), 0.0))
        um_s.append(um)
        for k in range(2):
            q = strips[k][side]
            after = roll(q, -1)
            edge = edge_sum(roll(q, 1), q, after, roll(q, -2))
            flux = flux_of(coefs, q, after, edge, roll(edge, 1), roll(edge, -1))
            edge_s[k].append(edge)
            flux_s[k].append(flux)
            star_s[k].append(q + roll(flux, 1) - flux)
    um_halo = jnp.where(low, um_s[0], um_s[1])
    edge_halo = [jnp.where(low, edge_s[k][0], edge_s[k][1]) for k in range(2)]
    for k in range(2):
        put(STRIP + k, jnp.where(low, star_s[k][0], star_s[k][1]))
    put(VM_S, jnp.where(low, vm_s[0], vm_s[1]))
    put(DEPTH_S, jnp.where(low, depth_s[0], depth_s[1]))
    put(METRIC_S, jnp.where(low, my_s[0], my_s[1]))

    head, tail, heads = lane == 0, lane == LANES - 1, lane < 2
    wet = [w_ref[l, rows, :] for l in range(LEVELS)]
    depth = sum(wet[1:], wet[0]).astype(F32)
    mx, my = mx_ref[rows, :], my_ref[rows, :]
    put(DEPTH, depth)
    put(METRIC, my)
    shallow = jnp.minimum(depth, roll(jnp.where(head, roll(depth_s[1], -4), depth), -1))
    for l in range(LEVELS):
        masked = [jnp.where(wet[l] != 0, field[l, rows, :], 0.0) for field in fields]
        um = masked[2] * mx
        put(VM + l, masked[3] * my)
        opening = shallow > float(l)
        place = 124 - 8 * l
        coefs = face_coefs(
            jnp.where(opening, 0.5 * (um + roll(jnp.where(head, roll(um_halo, place), um), -1)), 0.0)
        )
        for f in range(4):
            q, k = masked[f], f // 2
            place = 124 - 8 * ((f % 2) * 8 + l)
            h = roll(halo[k], place)
            after = roll(jnp.where(head, h, q), -1)
            edge = edge_sum(roll(jnp.where(tail, h, q), 1), q, after, roll(jnp.where(heads, h, q), -2))
            h = roll(edge_halo[k], place)
            flux = flux_of(
                coefs,
                q,
                after,
                edge,
                roll(jnp.where(tail, h, edge), 1),
                roll(jnp.where(head, h, edge), -1),
            )
            h = roll(flux_s[k][0], place)
            put(f * LEVELS + l, q + roll(jnp.where(tail, h, flux), 1) - flux)


def field_planes(strips):
    planes = [(p, p) for p in range(32)]
    return planes + [(STRIP, AD_STRIP), (STRIP + 1, AD_STRIP + 1)] if strips else planes


def all_edges(stack, edges, r, strips=True):
    for p, to in field_planes(strips):
        edges[to, pl.ds(r, TILE), :] = edge_sum(
            stack[p, pl.ds(r - 1, TILE), :],
            stack[p, pl.ds(r, TILE), :],
            stack[p, pl.ds(r + 1, TILE), :],
            stack[p, pl.ds(r + 2, TILE), :],
        )


def all_fluxes(stack, edges, fluxes, r, put_weight, strips=True):
    here, after = pl.ds(r, TILE), pl.ds(r + 1, TILE)

    def put(coefs, p, to):
        fluxes[to, here, :] = flux_of(
            coefs,
            stack[p, here, :],
            stack[p, after, :],
            edges[to, here, :],
            edges[to, pl.ds(r - 1, TILE), :],
            edges[to, after, :],
        )

    shallow = jnp.minimum(stack[DEPTH, here, :], stack[DEPTH, after, :])
    mean_metric = 0.5 * (stack[METRIC, here, :] + stack[METRIC, after, :])
    put_weight(shallow, mean_metric)
    for l in range(LEVELS):
        opening = shallow > float(l)
        coefs = face_coefs(jnp.where(opening, 0.5 * (stack[VM + l, here, :] + stack[VM + l, after, :]), 0.0))
        for f in range(4):
            put(coefs, f * LEVELS + l, f * LEVELS + l)
    if strips:
        level = ((iota(1) >> 3) & 7).astype(F32)
        opening = jnp.minimum(stack[DEPTH_S, here, :], stack[DEPTH_S, after, :]) > level
        coefs = face_coefs(jnp.where(opening, 0.5 * (stack[VM_S, here, :] + stack[VM_S, after, :]), 0.0))
        for k in range(2):
            put(coefs, STRIP + k, AD_STRIP + k)


def all_updates(stack, fluxes, advected, r, strips=True):
    here, before = pl.ds(r, TILE), pl.ds(r - 1, TILE)
    for p, to in field_planes(strips):
        advected[to, here, :] = stack[p, here, :] + fluxes[to, before, :] - fluxes[to, here, :]


def weights_to(ref, r, at=0):
    def put(shallow, mean_metric):
        ref[at, pl.ds(r, TILE), :] = shallow
        ref[at + 1, pl.ds(r, TILE), :] = mean_metric

    return put


def finish(advected, r, depth, weights, coupling, spreading, put):
    lane = iota(1)
    head, tail = lane == 0, lane == LANES - 1
    here, before, after = pl.ds(r, TILE), pl.ds(r - 1, TILE), pl.ds(r + 1, TILE)
    face = [(weights(0), weights(1)), (weights(2), weights(3))]
    face += [(advected[WY, at, :], advected[WY + 1, at, :]) for at in (here, before)]
    links, factors, inverses = [], [], []
    for l in range(LEVELS):
        divisor = jnp.ones((TILE, LANES), F32)
        if l < LEVELS - 1:
            links.append(jnp.where(depth > float(l + 1), coupling(l), 0.0))
            divisor = divisor + links[l]
        if l > 0:
            divisor = divisor + links[l - 1] - links[l - 1] * factors[l - 1]
        inverses.append(1.0 / divisor)
        if l < LEVELS - 1:
            factors.append(links[l] * inverses[l])
    for f in range(4):
        reduced = []
        for l in range(LEVELS):
            p = f * LEVELS + l
            x_up, x_down, y_up, y_down = (jnp.where(shallow > float(l), mean, 0.0) for shallow, mean in face)
            a = advected[p, here, :]
            h = roll(advected[AD_STRIP + f // 2, here, :], 124 - 8 * ((f % 2) * 8 + l))
            bend = (
                x_up * (roll(jnp.where(head, h, a), -1) - a)
                - x_down * (a - roll(jnp.where(tail, h, a), 1))
                + y_up * (advected[p, after, :] - a)
                - y_down * (a - advected[p, before, :])
            )
            target = a + spreading[f, l] * bend
            if l > 0:
                target = target + links[l - 1] * reduced[l - 1]
            reduced.append(target * inverses[l])
        solved = reduced[LEVELS - 1]
        put(f * LEVELS + LEVELS - 1, jnp.where(depth > float(LEVELS - 1), solved, 0.0))
        for l in range(LEVELS - 2, -1, -1):
            solved = reduced[l] + factors[l] * solved
            put(f * LEVELS + l, jnp.where(depth > float(l), solved, 0.0))


def edge_kernel(
    lat_ref, t_ref, s_ref, u_ref, v_ref, w_ref, mx_ref, my_ref, own_ref, ownx_ref, fromw_ref, frome_ref,
    a_ref, b_ref, edge_ref,
):
    fields = (t_ref, s_ref, u_ref, v_ref)
    tiles = mx_ref.shape[0] // TILE

    def sweep(e, carry):
        def put(p, x):
            edge_ref[e, p] = x

        x_tile(e * (tiles - 1), fields, w_ref, mx_ref, my_ref, own_ref, ownx_ref, fromw_ref, frome_ref, put)
        return carry

    lax.fori_loop(0, 2, sweep, 0)
    lane, sub = iota(1), iota(0)
    upper = sub < 4
    lat = lat_ref[0]
    even = (lat & 1) == 0
    fold = lat == lat_ref[1] - 1

    def send(k, lanes, first_sign, second_sign):
        one, two = 2 * k, 2 * k + 1
        bottom = jnp.where(upper, edge_ref[0, one], turn(edge_ref[0, two], 4))
        top = jnp.where(upper, turn(edge_ref[1, one], 4), edge_ref[1, two])
        mirror = jnp.where((sub & 1) != 0, turn(top, 1), turn(top, -1))
        mirror = jnp.where((sub & 2) != 0, turn(mirror, 2), turn(mirror, -2))
        mirror = jnp.take_along_axis(mirror, lanes, axis=1) * jnp.where(upper, first_sign, second_sign)
        a_ref[k] = jnp.where(even, top, bottom)
        b_ref[k] = jnp.where(even, bottom, jnp.where(fold, mirror, top))

    def send_plain(i, carry):
        for k in range(3):
            pair = i * 3 + k
            sign = jnp.where((pair >= 8) & (pair < 20), -1.0, 1.0)
            send(pair, LANES - 1 - lane, sign, sign)
        return carry

    lax.fori_loop(0, STRIP // 6, send_plain, 0)
    for e in range(2):
        edge_ref[e, PLANES] = jnp.zeros((TILE, LANES), F32)
    send(STRIP // 2, lane ^ 7, 1.0, -1.0)
    send(STRIP // 2 + 1, lane ^ 7, -1.0, 1.0)
    send(STRIP // 2 + 2, lane ^ 7, 1.0, 1.0)


def flip_kernel(t_ref, s_ref, u_ref, v_ref, w_ref, mx_ref, turned_ref, side_ref):
    fields = (t_ref, s_ref, u_ref, v_ref)

    def body(l, carry):
        wet = w_ref[l]
        for f in range(4):
            turned_ref[f * LEVELS + l] = jnp.where(wet != 0, fields[f][l], 0.0).T
        return carry + wet

    depth = lax.fori_loop(0, LEVELS, body, jnp.zeros(mx_ref.shape, jnp.int32))
    side_ref[0] = depth.astype(F32).T
    side_ref[1] = mx_ref[...].T


def interior_kernel(
    coef_ref, turned_ref, side_ref, v_ref, w_ref, my_ref, idf_ref, fromw_ref, frome_ref,
    o0, o1, o2, o3, adv_ref, weight_ref,
    wide, edges, fluxes, wide_star, halos, stack, advected, out, sems,
):
    outs = (o0, o1, o2, o3)
    rows_total, cols_total = my_ref.shape
    tiles, col_tiles = rows_total // TILE, cols_total // TILE
    margin = 2 * TILE
    inner = pl.ds(margin, cols_total)
    sub = iota(0)
    upper = sub < 4
    lane = lax.broadcasted_iota(jnp.int32, (rows_total, LANES), 1)
    low = (lane & 7) < 4
    every = pl.ds(0, rows_total)
    west, east = fromw_ref[every, :], frome_ref[every, :]
    for k, halo in enumerate((jnp.where(low, west, east), jnp.where(low, roll(west, -4), roll(east, 4)))):
        halos[pl.ds(k * 16, 16)] = halo.T.reshape(16, TILE, rows_total)
    third, fourth = pl.ds(rows_total + 2 * TILE, TILE), pl.ds(rows_total + 3 * TILE, TILE)
    depth_halo = jnp.where(upper, fromw_ref[third, :], frome_ref[third, :])
    mx_halo = jnp.where(upper, turn(fromw_ref[third, :], 4), turn(frome_ref[third, :], 4))
    my_halo = jnp.where(upper, fromw_ref[fourth, :], frome_ref[fourth, :])

    def fill(p, middle, halo):
        halo = turn(halo, 4)
        wide[p, pl.ds(TILE, TILE), :] = halo
        wide[p, pl.ds(margin + cols_total, TILE), :] = halo
        wide[p, inner, :] = middle

    def fill_field(p, carry):
        fill(p, turned_ref[p], halos[p])
        return carry

    lax.fori_loop(0, 32, fill_field, 0)
    fill(DEPTH, side_ref[0], depth_halo)
    fill(METRIC, side_ref[1], mx_halo)

    def sweep_wide_edges(j, carry):
        r = pl.multiple_of(j * TILE, TILE)
        here = pl.ds(r, TILE)
        metric = wide[METRIC, here, :]
        for l in range(LEVELS):
            wide[VM + l, here, :] = wide[2 * LEVELS + l, here, :] * metric
        all_edges(wide, edges, r, False)
        return carry

    def sweep_wide(j, carry):
        r = pl.multiple_of(j * TILE, TILE)

        def put(shallow, mean_metric):
            for k, at in enumerate((r, r + 1)):
                wide_star[FACES + 2 * k, pl.ds(at, TILE), :] = shallow
                wide_star[FACES + 2 * k + 1, pl.ds(at, TILE), :] = mean_metric

        all_fluxes(wide, edges, fluxes, r, put, False)
        all_updates(wide, fluxes, wide_star, r, False)
        return carry

    lax.fori_loop(1, col_tiles + 3, sweep_wide_edges, 0)
    lax.fori_loop(1, col_tiles + 3, sweep_wide, 0)

    def sweep_strips(p, carry):
        rows = pl.ds(pl.multiple_of(margin + p * TILE, TILE), TILE)
        for k in range(2):
            left = wide_star[p + 16 * k, pl.ds(TILE, TILE), :]
            right = wide_star[p + 16 * k, pl.ds(margin + cols_total, TILE), :]
            wide_star[32 + k, rows, :] = jnp.where(sub == 3, turn(left, 4), turn(right, 4))
        wide_star[34, rows, :] = halos[3 * LEVELS + (p & 7)] * my_halo
        wide_star[35, rows, :] = depth_halo
        wide_star[36, rows, :] = my_halo
        return carry

    lax.fori_loop(0, 16, sweep_strips, 0)
    body_rows = pl.ds(TILE, rows_total)

    def sweep_back(i, carry):
        for k in range(4):
            p = i * 4 + k
            stack[p + (STRIP - 32) * (p >= 32).astype(jnp.int32), body_rows, :] = wide_star[p, inner, :].T
        return carry

    lax.fori_loop(0, TURNED // 4, sweep_back, 0)

    def sweep_own(t, carry):
        start = pl.multiple_of(t * TILE, TILE)
        rows, here = pl.ds(start, TILE), pl.ds(start + TILE, TILE)
        my = my_ref[rows, :]
        depth = w_ref[0, rows, :]
        for l in range(1, LEVELS):
            depth = depth + w_ref[l, rows, :]
        stack[DEPTH, here, :] = depth.astype(F32)
        stack[METRIC, here, :] = my
        for l in range(LEVELS):
            stack[VM + l, here, :] = jnp.where(w_ref[l, rows, :] != 0, v_ref[l, rows, :], 0.0) * my
        all_edges(stack, edges, start + TILE)
        return carry

    def sweep_y(t, carry):
        r = pl.multiple_of(t * TILE + TILE, TILE)
        all_fluxes(stack, edges, fluxes, r, weights_to(advected, r, WY))
        all_updates(stack, fluxes, advected, r)
        return carry

    def copies(t_rows):
        return [
            pltpu.make_async_copy(out.at[pl.ds(f * LEVELS, LEVELS), t_rows, :], outs[f].at[:, t_rows, :], sems.at[f])
            for f in range(4)
        ]

    def sweep_out(t, carry):
        start = pl.multiple_of(t * TILE, TILE)
        rows = pl.ds(start, TILE)
        depth = stack[DEPTH, pl.ds(start + TILE, TILE), :]

        def put(p, x):
            out[p, rows, :] = x

        finish(
            advected, pl.multiple_of(start + TILE, TILE), depth,
            lambda i: stack[PLANES + i, pl.ds(start + TILE, TILE), :], lambda l: idf_ref[l, rows, :], coef_ref, put,
        )
        for copy in copies(rows):
            copy.start()
        return carry

    lax.fori_loop(0, tiles, sweep_own, 0)
    lax.fori_loop(0, tiles, sweep_y, 0)
    lax.fori_loop(1, tiles - 1, sweep_out, 0)
    for e, start in enumerate((0, rows_total - 2 * TILE)):
        adv_ref[:, pl.ds(e * 2 * TILE, 2 * TILE), :] = advected[:, pl.ds(start + TILE, 2 * TILE), :]
    for e, start in enumerate((0, rows_total - TILE)):
        weight_ref[e] = stack[pl.ds(PLANES, 4), pl.ds(start + TILE, TILE), :]
    for copy in copies(pl.ds(TILE, rows_total - 2 * TILE)):
        copy.wait()


def border_kernel(
    lat_ref, coef_ref, idf_lo, idf_hi, a_ref, b_ref, edge_ref, adv_ref, weight_ref, i0, i1, i2, i3,
    o0, o1, o2, o3,
    stack, edges, fluxes, advected, out, sems,
):
    outs = (o0, o1, o2, o3)
    rows_total = o0.shape[1]
    even = (lat_ref[0] & 1) == 0
    started = []
    for e in range(2):
        for p in range(PLANES):
            k = p // 2
            if e == 0:
                halo = jnp.where(even, b_ref[k], a_ref[k])
                stack[p, pl.ds(0, TILE), :] = turn(halo, 4) if p % 2 == 0 else halo
            else:
                halo = jnp.where(even, a_ref[k], b_ref[k])
                stack[p, pl.ds(2 * TILE, TILE), :] = halo if p % 2 == 0 else turn(halo, 4)
            stack[p, pl.ds(TILE, TILE), :] = edge_ref[e, p]
        advected[:, pl.ds(TILE if e == 0 else 0, 2 * TILE), :] = adv_ref[:, pl.ds(e * 2 * TILE, 2 * TILE), :]
        all_edges(stack, edges, 5 if e == 0 else 11)
        face = 6 if e == 0 else 12
        all_fluxes(stack, edges, fluxes, face, weights_to(advected, face, WY))
        all_updates(stack, fluxes, advected, 3 if e == 0 else 13)

        def put(p, x, e=e):
            out[e, p] = x

        idf = idf_lo if e == 0 else idf_hi
        finish(
            advected, TILE, stack[DEPTH, pl.ds(TILE, TILE), :],
            lambda p, e=e: weight_ref[e, p], lambda l, idf=idf: idf[l], coef_ref, put,
        )
        rows = pl.ds(0 if e == 0 else rows_total - TILE, TILE)
        for f in range(4):
            copy = pltpu.make_async_copy(
                out.at[e, pl.ds(f * LEVELS, LEVELS)], outs[f].at[:, rows, :], sems.at[e, f]
            )
            copy.start()
            started.append(copy)
    for copy in started:
        copy.wait()


def vmem(n):
    return [pl.BlockSpec(memory_space=pltpu.VMEM)] * n


def anywhere(n):
    return [pl.BlockSpec(memory_space=pl.ANY)] * n


def smem(n):
    return [pl.BlockSpec(memory_space=pltpu.SMEM)] * n


def shape(*dims):
    return jax.ShapeDtypeStruct(dims, F32)


PARAMS = pltpu.CompilerParams(vmem_limit_bytes=40 * 1024 * 1024)


def call_pack(base):
    rows, cols = base[5].shape
    steps = 2
    part = rows // steps
    wide = lambda: pl.BlockSpec((LEVELS, part, cols), lambda i: (0, i, 0))
    flat = lambda: pl.BlockSpec((rows, cols), lambda i: (0, 0))
    return pl.pallas_call(
        pack_kernel,
        grid=(steps,),
        out_shape=(shape(2, rows, LANES), shape(3, TILE, LANES), shape(rows + 4 * TILE, LANES), shape(rows + 4 * TILE, LANES)),
        in_specs=[wide() for _ in range(5)] + [flat(), flat()],
        scratch_shapes=[pltpu.VMEM((rows, LANES), F32)],
        out_specs=(
            pl.BlockSpec((2, part, LANES), lambda i: (0, i, 0)),
            pl.BlockSpec((3, TILE, LANES), lambda i: (0, 0, 0)),
            pl.BlockSpec((rows + 4 * TILE, LANES), lambda i: (0, 0)),
            pl.BlockSpec((rows + 4 * TILE, LANES), lambda i: (0, 0)),
        ),
    )(*base)


def call_edge(lat_info, base, sides):
    return pl.pallas_call(
        edge_kernel,
        out_shape=(shape(PAIRS, TILE, LANES), shape(PAIRS, TILE, LANES), shape(2, 2 * PAIRS, TILE, LANES)),
        in_specs=smem(1) + vmem(11),
        out_specs=tuple(vmem(3)),
        compiler_params=PARAMS,
    )(lat_info, *base, *sides)


def call_flip(base):
    rows, cols = base[5].shape
    return pl.pallas_call(
        flip_kernel,
        out_shape=(shape(32, cols, rows), shape(2, cols, rows)),
        in_specs=vmem(6),
        out_specs=tuple(vmem(2)),
        compiler_params=PARAMS,
        cost_estimate=pl.CostEstimate(flops=8_000_000, bytes_accessed=5_000_000, transcendentals=0),
    )(*base[:6])


def call_interior(spreading, turned, side, north, water, metric_y, diffusion, from_west, from_east):
    rows, cols = metric_y.shape
    stack_rows = rows + 2 * TILE
    wide_rows = cols + 4 * TILE
    return pl.pallas_call(
        interior_kernel,
        out_shape=(shape(LEVELS, rows, cols),) * 4 + (shape(AD_PLANES, 4 * TILE, LANES), shape(2, 4, TILE, LANES)),
        in_specs=smem(1) + vmem(8),
        out_specs=tuple(anywhere(4) + vmem(2)),
        scratch_shapes=[
            pltpu.VMEM((STRIP, wide_rows, rows), F32),
            pltpu.VMEM((34, wide_rows, LANES), F32),
            pltpu.VMEM((34, wide_rows, LANES), F32),
            pltpu.VMEM((TURNED, wide_rows, rows), F32),
            pltpu.VMEM((32, TILE, rows), F32),
            pltpu.VMEM((TURNED + STRIP - 32, stack_rows, LANES), F32),
            pltpu.VMEM((AD_PLANES, stack_rows, LANES), F32),
            pltpu.VMEM((32, rows, LANES), F32),
            pltpu.SemaphoreType.DMA((4,)),
        ],
        compiler_params=PARAMS,
    )(spreading, turned, side, north, water, metric_y, diffusion, from_west, from_east)


def call_border(lat_info, spreading, diffusion, got_a, got_b, edge, advected, weights, outs):
    _, rows, cols = outs[0].shape
    last = rows // TILE - 1
    return pl.pallas_call(
        border_kernel,
        grid=(1,),
        out_shape=(shape(LEVELS, rows, cols),) * 4,
        in_specs=smem(2)
        + [
            pl.BlockSpec((LEVELS - 1, TILE, cols), lambda i: (0, 0, 0)),
            pl.BlockSpec((LEVELS - 1, TILE, cols), lambda i: (0, last, 0)),
        ]
        + vmem(5)
        + anywhere(4),
        out_specs=tuple(anywhere(4)),
        scratch_shapes=[
            pltpu.VMEM((PLANES, 3 * TILE, LANES), F32),
            pltpu.VMEM((34, 3 * TILE, LANES), F32),
            pltpu.VMEM((34, 3 * TILE, LANES), F32),
            pltpu.VMEM((AD_PLANES, 3 * TILE, LANES), F32),
            pltpu.VMEM((2, 32, TILE, LANES), F32),
            pltpu.SemaphoreType.DMA((2, 4)),
        ],
        input_output_aliases={9 + f: f for f in range(4)},
        compiler_params=PARAMS,
    )(lat_info, spreading, diffusion, diffusion, got_a, got_b, edge, advected, weights, *outs)


def shards(heat, salt, east, north, water, metric_x, metric_y, diffusion, spreading, mirror):
    cols = metric_x.shape[1]
    lon_count, lat_count = lax.axis_size("lon"), lax.axis_size("lat")
    lon, lat = lax.axis_index("lon"), lax.axis_index("lat")
    lat_info = jnp.stack([lat, jnp.int32(lat_count)]).astype(jnp.int32)
    pivot = (mirror[0] // cols + lon) % lon_count

    base = (heat, salt, east, north, water, metric_x, metric_y)
    own, ownx, to_east, to_west = call_pack(base)
    ring = [(i, (i + 1) % lon_count) for i in range(lon_count)]
    from_west = lax.ppermute(to_east, "lon", ring)
    from_east = lax.ppermute(to_west, "lon", [(j, i) for i, j in ring])
    turned, side = call_flip(base)
    sides = (own, ownx, from_west, from_east)
    rows_a, rows_b, edge = call_edge(lat_info, base, sides)

    index = lambda o, a: o * lat_count + a
    pairs = [(index(o, a), index(o, a ^ 1)) for o in range(lon_count) for a in range(lat_count)]
    got_a = lax.ppermute(rows_a, ("lon", "lat"), pairs)

    def across(k, x):
        fixed = []
        for o in range(lon_count):
            for a in range(1, lat_count - 1):
                fixed.append((index(o, a), index(o, ((a + 1) ^ 1) - 1)))
            fixed.append((index(o, lat_count - 1), index((k - o) % lon_count, lat_count - 1)))
        got = lax.ppermute(x, ("lon", "lat"), fixed)
        return got, interior(spreading, turned, side, north, water, metric_y, diffusion, from_west, from_east)

    interior = jax.jit(call_interior)
    got_b, results = lax.switch(pivot, [functools.partial(across, k) for k in range(lon_count)], rows_b)
    return call_border(lat_info, spreading, diffusion, got_a, got_b, edge, results[4], results[5], results[:4])


def solution(mesh):
    block = P(None, "lat", "lon")
    in_specs = (block,) * 5 + (P("lat", "lon"),) * 2 + (block, P(), P("lon"))
    return jax.shard_map(shards, mesh=mesh, in_specs=in_specs, out_specs=(block,) * 4, check_vma=False)
```

```python
import functools
import jax
import jax.numpy as jnp
from jax import lax
from jax.experimental import pallas as pl
from jax.experimental.pallas import tpu as pltpu
from jax.sharding import PartitionSpec as P

F32 = jnp.float32
LEVELS = 8
TILE = 8
LANES = 128
VM, DEPTH, METRIC, STRIP, VM_S, DEPTH_S, METRIC_S, PLANES = 32, 40, 41, 42, 44, 45, 46, 47
PAIRS = 24
AD_STRIP, WY, AD_PLANES = 32, 34, 36


def roll(x, shift):
    shift %= LANES
    return x if shift == 0 else pltpu.roll(x, shift, 1)


def turn(x, shift):
    return pltpu.roll(x, shift % TILE, 0)


def iota(dimension):
    return lax.broadcasted_iota(jnp.int32, (TILE, LANES), dimension)


def face_coefs(courant):
    size = jnp.abs(courant)
    rest = 1.0 - size
    edge = courant * rest * (1.0 / 12.0)
    return edge * rest, courant * size * (3.0 - 2.0 * size), edge * size, courant >= 0.0


def edge_sum(before, here, after, beyond):
    return 7.0 * (here + after) - (before + beyond)


def flux_of(coefs, here, after, edge, edge_before, edge_after):
    own, centre, far, positive = coefs
    return own * edge + centre * jnp.where(positive, here, after) - far * jnp.where(positive, edge_before, edge_after)


def pack_kernel(t_ref, s_ref, u_ref, v_ref, w_ref, mx_ref, my_ref, toe_ref, tow_ref, depths, ownx_ref):
    fields = (t_ref, s_ref, u_ref, v_ref)
    step, tiles = pl.program_id(0), t_ref.shape[1] // TILE
    rows_total = mx_ref.shape[0]
    lane = iota(1)
    low = (lane & 7) < 4
    group = lane >> 3
    zero = jnp.zeros((TILE, LANES), F32)

    @pl.when(step == 0)
    def _():
        for i in range(3):
            ownx_ref[i] = zero

    def body(t, carry):
        rows = pl.ds(pl.multiple_of(t * TILE, TILE), TILE)
        tile = t + step * tiles
        whole = pl.ds(pl.multiple_of(tile * TILE, TILE), TILE)
        wet = [w_ref[l, rows, :] for l in range(LEVELS)]
        depth = sum(wet[1:], wet[0]).astype(F32)
        packs = []
        for k in range(2):
            pack = zero
            for p in range(16):
                q = jnp.where(wet[p % 8] != 0, fields[2 * k + p // 8][p % 8, rows, :], 0.0)
                pack = jnp.where(group == p, roll(q, 4 + 8 * p), pack)
            packs.append(pack)
        toe_ref[whole, :] = jnp.where(low, packs[0], roll(packs[1], 4))
        tow_ref[whole, :] = jnp.where(low, roll(packs[1], -4), packs[0])
        shift = (4 + 8 * tile) & (LANES - 1)
        depths[whole, :] = depth
        for i, x in enumerate((depth, mx_ref[whole, :], my_ref[whole, :])):
            ownx_ref[i] = jnp.where(group == tile, pltpu.roll(x, shift, 1), ownx_ref[i])
        return carry

    lax.fori_loop(0, tiles, body, 0)

    @pl.when(step == pl.num_programs(0) - 1)
    def _():
        depth, metric_x, metric_y = ownx_ref[0], ownx_ref[1], ownx_ref[2]
        first, second = pl.ds(rows_total, TILE), pl.ds(rows_total + TILE, TILE)
        toe_ref[first, :] = jnp.where(low, depth, roll(metric_x, 4))
        toe_ref[second, :] = jnp.where(low, metric_y, 0.0)
        tow_ref[first, :] = jnp.where(low, roll(metric_x, -4), depth)
        tow_ref[second, :] = jnp.where(low, 0.0, metric_y)
        upper = iota(0) < 4
        turned = [x[...].T for x in (depths, mx_ref, my_ref)]
        starts = [x[:TILE] for x in turned]
        ends = [x[-TILE:] for x in turned]
        third, fourth = pl.ds(rows_total + 2 * TILE, TILE), pl.ds(rows_total + 3 * TILE, TILE)
        toe_ref[third, :] = jnp.where(upper, turn(ends[0], 4), ends[1])
        tow_ref[third, :] = jnp.where(upper, starts[1], turn(starts[0], 4))
        toe_ref[fourth, :] = jnp.where(upper, turn(ends[2], 4), 0.0)
        tow_ref[fourth, :] = jnp.where(upper, 0.0, turn(starts[2], 4))


def x_tile(t, fields, w_ref, mx_ref, my_ref, fromw_ref, frome_ref, put):
    rows_total = mx_ref.shape[0]
    start = pl.multiple_of(t * TILE, TILE)
    rows = pl.ds(start, TILE)
    lane = iota(1)
    low = (lane & 7) < 4
    group = lane >> 3
    level = (group & 7).astype(F32)
    half = lane < 64
    west, east = fromw_ref[rows, :], frome_ref[rows, :]
    halo = (jnp.where(low, west, east), jnp.where(low, roll(west, -4), roll(east, 4)))
    wet = [w_ref[l, rows, :] for l in range(LEVELS)]
    depth = sum(wet[1:], wet[0]).astype(F32)
    mx, my = mx_ref[rows, :], my_ref[rows, :]
    own = []
    for k in range(2):
        pack = jnp.zeros((TILE, LANES), F32)
        for p in range(16):
            q = jnp.where(wet[p % 8] != 0, fields[2 * k + p // 8][p % 8, rows, :], 0.0)
            pack = jnp.where(group == p, roll(q, 4 + 8 * p), pack)
        own.append(pack)
    strips = [(jnp.where(low, halo[k], own[k]), jnp.where(low, own[k], halo[k])) for k in range(2)]
    first, second = pl.ds(rows_total, TILE), pl.ds(rows_total + TILE, TILE)
    west, east = fromw_ref[first, :], frome_ref[first, :]
    west_2, east_2 = fromw_ref[second, :], frome_ref[second, :]
    side_halo = (
        jnp.where(low, west, east),
        jnp.where(low, roll(west, -4), roll(east, 4)),
        jnp.where(low, west_2, east_2),
    )

    def spread(x):
        x = jnp.where(group == t, x, 0.0)
        for shift in (8, 16, 32, 64):
            x = x + roll(x, shift)
        return x

    extra = []
    for i, mine in enumerate((depth, mx, my)):
        mine = pltpu.roll(mine, (4 + 8 * t) & (LANES - 1), 1)
        extra.append((spread(jnp.where(low, side_halo[i], mine)), spread(jnp.where(low, mine, side_halo[i]))))
    depth_s, mx_s, my_s = extra

    um_s, edge_s, flux_s, star_s, vm_s = [], [[], []], [[], []], [[], []], []
    for side in range(2):
        mixed = strips[1][side]
        swapped = roll(mixed, 64)
        um = jnp.where(half, mixed, swapped) * mx_s[side]
        vm_s.append(jnp.where(half, swapped, mixed) * my_s[side])
        opening = jnp.minimum(depth_s[side], roll(depth_s[side], -1)) > level
        coefs = face_coefs(jnp.where(opening, 0.5 * (um + roll(um, -1)), 0.0))
        um_s.append(um)
        for k in range(2):
            q = strips[k][side]
            after = roll(q, -1)
            edge = edge_sum(roll(q, 1), q, after, roll(q, -2))
            flux = flux_of(coefs, q, after, edge, roll(edge, 1), roll(edge, -1))
            edge_s[k].append(edge)
            flux_s[k].append(flux)
            star_s[k].append(q + roll(flux, 1) - flux)
    um_halo = jnp.where(low, um_s[0], um_s[1])
    edge_halo = [jnp.where(low, edge_s[k][0], edge_s[k][1]) for k in range(2)]
    for k in range(2):
        put(STRIP + k, jnp.where(low, star_s[k][0], star_s[k][1]))
    put(VM_S, jnp.where(low, vm_s[0], vm_s[1]))
    put(DEPTH_S, jnp.where(low, depth_s[0], depth_s[1]))
    put(METRIC_S, jnp.where(low, my_s[0], my_s[1]))

    head, tail, heads = lane == 0, lane == LANES - 1, lane < 2
    put(DEPTH, depth)
    put(METRIC, my)
    shallow = jnp.minimum(depth, roll(jnp.where(head, roll(depth_s[1], -4), depth), -1))
    for l in range(LEVELS):
        masked = [jnp.where(wet[l] != 0, field[l, rows, :], 0.0) for field in fields]
        um = masked[2] * mx
        put(VM + l, masked[3] * my)
        opening = shallow > float(l)
        place = 124 - 8 * l
        coefs = face_coefs(
            jnp.where(opening, 0.5 * (um + roll(jnp.where(head, roll(um_halo, place), um), -1)), 0.0)
        )
        for f in range(4):
            q, k = masked[f], f // 2
            place = 124 - 8 * ((f % 2) * 8 + l)
            h = roll(halo[k], place)
            after = roll(jnp.where(head, h, q), -1)
            edge = edge_sum(roll(jnp.where(tail, h, q), 1), q, after, roll(jnp.where(heads, h, q), -2))
            h = roll(edge_halo[k], place)
            flux = flux_of(
                coefs,
                q,
                after,
                edge,
                roll(jnp.where(tail, h, edge), 1),
                roll(jnp.where(head, h, edge), -1),
            )
            h = roll(flux_s[k][0], place)
            put(f * LEVELS + l, q + roll(jnp.where(tail, h, flux), 1) - flux)


def field_planes(strips):
    planes = [(p, p) for p in range(32)]
    return planes + [(STRIP, AD_STRIP), (STRIP + 1, AD_STRIP + 1)] if strips else planes


def all_edges(stack, edges, r, strips=True):
    for p, to in field_planes(strips):
        edges[to, pl.ds(r, TILE), :] = edge_sum(
            stack[p, pl.ds(r - 1, TILE), :],
            stack[p, pl.ds(r, TILE), :],
            stack[p, pl.ds(r + 1, TILE), :],
            stack[p, pl.ds(r + 2, TILE), :],
        )


def speed_times_metric(stack, r):
    here = pl.ds(r, TILE)
    metric = stack[METRIC, here, :]
    for l in range(LEVELS):
        stack[VM + l, here, :] = stack[2 * LEVELS + l, here, :] * metric


def all_fluxes(stack, edges, fluxes, r, put_weight, strips=True):
    here, after = pl.ds(r, TILE), pl.ds(r + 1, TILE)

    def put(coefs, p, to):
        fluxes[to, here, :] = flux_of(
            coefs,
            stack[p, here, :],
            stack[p, after, :],
            edges[to, here, :],
            edges[to, pl.ds(r - 1, TILE), :],
            edges[to, after, :],
        )

    shallow = jnp.minimum(stack[DEPTH, here, :], stack[DEPTH, after, :])
    mean_metric = 0.5 * (stack[METRIC, here, :] + stack[METRIC, after, :])
    put_weight(shallow, mean_metric)
    for l in range(LEVELS):
        opening = shallow > float(l)
        coefs = face_coefs(jnp.where(opening, 0.5 * (stack[VM + l, here, :] + stack[VM + l, after, :]), 0.0))
        for f in range(4):
            put(coefs, f * LEVELS + l, f * LEVELS + l)
    if strips:
        level = ((iota(1) >> 3) & 7).astype(F32)
        opening = jnp.minimum(stack[DEPTH_S, here, :], stack[DEPTH_S, after, :]) > level
        coefs = face_coefs(jnp.where(opening, 0.5 * (stack[VM_S, here, :] + stack[VM_S, after, :]), 0.0))
        for k in range(2):
            put(coefs, STRIP + k, AD_STRIP + k)


def all_updates(stack, fluxes, advected, r, strips=True):
    here, before = pl.ds(r, TILE), pl.ds(r - 1, TILE)
    for p, to in field_planes(strips):
        advected[to, here, :] = stack[p, here, :] + fluxes[to, before, :] - fluxes[to, here, :]


def weights_to(ref, r, at=0):
    def put(shallow, mean_metric):
        ref[at, pl.ds(r, TILE), :] = shallow
        ref[at + 1, pl.ds(r, TILE), :] = mean_metric

    return put


def finish(advected, r, depth, weights, coupling, spreading, put):
    lane = iota(1)
    head, tail = lane == 0, lane == LANES - 1
    here, before, after = pl.ds(r, TILE), pl.ds(r - 1, TILE), pl.ds(r + 1, TILE)
    face = [(weights(0), weights(1)), (weights(2), weights(3))]
    face += [(advected[WY, at, :], advected[WY + 1, at, :]) for at in (here, before)]
    links, factors, inverses = [], [], []
    for l in range(LEVELS):
        divisor = jnp.ones((TILE, LANES), F32)
        if l < LEVELS - 1:
            links.append(jnp.where(depth > float(l + 1), coupling(l), 0.0))
            divisor = divisor + links[l]
        if l > 0:
            divisor = divisor + links[l - 1] - links[l - 1] * factors[l - 1]
        inverses.append(1.0 / divisor)
        if l < LEVELS - 1:
            factors.append(links[l] * inverses[l])
    for f in range(4):
        reduced = []
        for l in range(LEVELS):
            p = f * LEVELS + l
            x_up, x_down, y_up, y_down = (jnp.where(shallow > float(l), mean, 0.0) for shallow, mean in face)
            a = advected[p, here, :]
            h = roll(advected[AD_STRIP + f // 2, here, :], 124 - 8 * ((f % 2) * 8 + l))
            bend = (
                x_up * (roll(jnp.where(head, h, a), -1) - a)
                - x_down * (a - roll(jnp.where(tail, h, a), 1))
                + y_up * (advected[p, after, :] - a)
                - y_down * (a - advected[p, before, :])
            )
            target = a + spreading[f, l] * bend
            if l > 0:
                target = target + links[l - 1] * reduced[l - 1]
            reduced.append(target * inverses[l])
        solved = reduced[LEVELS - 1]
        put(f * LEVELS + LEVELS - 1, jnp.where(depth > float(LEVELS - 1), solved, 0.0))
        for l in range(LEVELS - 2, -1, -1):
            solved = reduced[l] + factors[l] * solved
            put(f * LEVELS + l, jnp.where(depth > float(l), solved, 0.0))


def edge_kernel(
    lat_ref, t_ref, s_ref, u_ref, v_ref, w_ref, mx_ref, my_ref, fromw_ref, frome_ref, order_ref,
    a_ref, b_ref, edge_ref,
):
    fields = (t_ref, s_ref, u_ref, v_ref)
    tiles = mx_ref.shape[0] // TILE

    def sweep(e, carry):
        def put(p, x):
            edge_ref[e, p] = x

        x_tile(e * (tiles - 1), fields, w_ref, mx_ref, my_ref, fromw_ref, frome_ref, put)
        return carry

    lax.fori_loop(0, 2, sweep, 0)
    lane, sub = iota(1), iota(0)
    upper = sub < 4
    lat = lat_ref[0]
    even = (lat & 1) == 0
    fold = lat == lat_ref[1] - 1

    def send(k, lanes, first_sign, second_sign):
        one, two = 2 * k, 2 * k + 1
        bottom = jnp.where(upper, edge_ref[0, one], turn(edge_ref[0, two], 4))
        top = jnp.where(upper, turn(edge_ref[1, one], 4), edge_ref[1, two])
        mirror = jnp.where((sub & 1) != 0, turn(top, 1), turn(top, -1))
        mirror = jnp.where((sub & 2) != 0, turn(mirror, 2), turn(mirror, -2))
        mirror = jnp.take_along_axis(mirror, lanes, axis=1) * jnp.where(upper, first_sign, second_sign)
        a_ref[k] = jnp.where(even, top, bottom)
        b_ref[k] = jnp.where(even, bottom, jnp.where(fold, mirror, top))

    def send_plain(i, carry):
        for k in range(3):
            pair = i * 3 + k
            sign = jnp.where((pair >= 8) & (pair < 20), -1.0, 1.0)
            send(pair, LANES - 1 - lane, sign, sign)
        return carry

    lax.fori_loop(0, STRIP // 6, send_plain, 0)
    for e in range(2):
        edge_ref[e, PLANES] = jnp.zeros((TILE, LANES), F32)
    send(STRIP // 2, lane ^ 7, 1.0, -1.0)
    send(STRIP // 2 + 1, lane ^ 7, -1.0, 1.0)
    send(STRIP // 2 + 2, lane ^ 7, 1.0, 1.0)


def flip_kernel(
    t_ref, s_ref, u_ref, v_ref, w_ref, mx_ref, brink_ref, star_ref, side_ref, wide, edges, fluxes
):
    fields = (t_ref, s_ref, u_ref, v_ref)
    cols_total = mx_ref.shape[1]
    inner = pl.ds(TILE, cols_total)

    def body(l, carry):
        wet = w_ref[l]
        for f in range(4):
            wide[f * LEVELS + l, inner, :] = jnp.where(wet != 0, fields[f][l], 0.0).T
        return carry + wet

    depth = lax.fori_loop(0, LEVELS, body, jnp.zeros(mx_ref.shape, jnp.int32))
    for i, x in enumerate((depth.astype(F32).T, mx_ref[...].T)):
        side_ref[i] = x
        wide[DEPTH + i, inner, :] = x

    def sweep_edges(j, carry):
        r = pl.multiple_of(j * TILE + TILE, TILE)
        speed_times_metric(wide, r)
        all_edges(wide, edges, r, False)
        return carry

    def sweep(j, carry):
        r = pl.multiple_of(j * TILE + TILE, TILE)
        all_fluxes(wide, edges, fluxes, r, lambda shallow, mean_metric: None, False)
        all_updates(wide, fluxes, star_ref, r, False)
        return carry

    lax.fori_loop(0, cols_total // TILE, sweep_edges, 0)
    lax.fori_loop(0, cols_total // TILE, sweep, 0)
    brink_ref[:, pl.ds(0, 2 * TILE), :] = wide[pl.ds(0, 32), pl.ds(TILE, 2 * TILE), :]
    brink_ref[:, pl.ds(2 * TILE, 2 * TILE), :] = wide[pl.ds(0, 32), pl.ds(cols_total - TILE, 2 * TILE), :]


def interior_kernel(
    coef_ref, brink_ref, star_ref, side_ref, v_ref, w_ref, my_ref, idf_ref, fromw_ref, frome_ref,
    o0, o1, o2, o3, adv_ref, weight_ref,
    wide, edges, fluxes, wide_star, side_wide, extra, halos, stack, advected, out, sems,
):
    outs = (o0, o1, o2, o3)
    rows_total, cols_total = my_ref.shape
    tiles, col_tiles = rows_total // TILE, cols_total // TILE
    margin = 2 * TILE
    inner = pl.ds(margin, cols_total)
    sub = iota(0)
    upper = sub < 4
    lane = lax.broadcasted_iota(jnp.int32, (rows_total, LANES), 1)
    low = (lane & 7) < 4
    every = pl.ds(0, rows_total)
    west, east = fromw_ref[every, :], frome_ref[every, :]
    for k, halo in enumerate((jnp.where(low, west, east), jnp.where(low, roll(west, -4), roll(east, 4)))):
        halos[pl.ds(k * 16, 16)] = halo.T.reshape(16, TILE, rows_total)
    third, fourth = pl.ds(rows_total + 2 * TILE, TILE), pl.ds(rows_total + 3 * TILE, TILE)
    depth_halo = jnp.where(upper, fromw_ref[third, :], frome_ref[third, :])
    mx_halo = jnp.where(upper, turn(fromw_ref[third, :], 4), turn(frome_ref[third, :], 4))
    my_halo = jnp.where(upper, fromw_ref[fourth, :], frome_ref[fourth, :])

    def fill(p, first, last, halo):
        halo = turn(halo, 4)
        wide[p, pl.ds(TILE, TILE), :] = halo
        wide[p, pl.ds(2 * TILE, 2 * TILE), :] = first
        wide[p, pl.ds(5 * TILE, 2 * TILE), :] = last
        wide[p, pl.ds(7 * TILE, TILE), :] = halo

    def fill_field(p, carry):
        fill(p, brink_ref[p, pl.ds(0, 2 * TILE), :], brink_ref[p, pl.ds(2 * TILE, 2 * TILE), :], halos[p])
        return carry

    lax.fori_loop(0, 32, fill_field, 0)
    for i, halo in enumerate((depth_halo, mx_halo)):
        end = pl.ds(cols_total - 2 * TILE, 2 * TILE)
        fill(DEPTH + i, side_ref[i, pl.ds(0, 2 * TILE), :], side_ref[i, end, :], halo)
        side_wide[i, pl.ds(TILE, TILE), :] = turn(halo, 4)
        side_wide[i, inner, :] = side_ref[i]
        side_wide[i, pl.ds(margin + cols_total, TILE), :] = turn(halo, 4)

    def place(j):
        return pl.multiple_of(TILE + j * TILE + TILE * (j >= 3).astype(jnp.int32), TILE)

    def sweep_wide_edges(j, carry):
        speed_times_metric(wide, place(j))
        all_edges(wide, edges, place(j), False)
        return carry

    def sweep_wide(j, carry):
        all_fluxes(wide, edges, fluxes, place(j), lambda shallow, mean_metric: None, False)
        all_updates(wide, fluxes, wide_star, place(j), False)
        return carry

    def sweep_faces(j, carry):
        r = pl.multiple_of(j * TILE, TILE)
        here, after = pl.ds(r, TILE), pl.ds(r + 1, TILE)
        shallow = jnp.minimum(side_wide[0, here, :], side_wide[0, after, :])
        mean_metric = 0.5 * (side_wide[1, here, :] + side_wide[1, after, :])
        for k, at in enumerate((here, after)):
            extra[5 + 2 * k, at, :] = shallow
            extra[6 + 2 * k, at, :] = mean_metric
        return carry

    lax.fori_loop(0, 6, sweep_wide_edges, 0)
    lax.fori_loop(0, 6, sweep_wide, 0)
    lax.fori_loop(1, col_tiles + 2, sweep_faces, 0)

    def sweep_strips(p, carry):
        rows = pl.ds(pl.multiple_of(margin + p * TILE, TILE), TILE)
        for k in range(2):
            left = wide_star[p + 16 * k, pl.ds(TILE, TILE), :]
            right = wide_star[p + 16 * k, pl.ds(7 * TILE, TILE), :]
            extra[k, rows, :] = jnp.where(sub == 3, turn(left, 4), turn(right, 4))
        extra[2, rows, :] = halos[3 * LEVELS + (p & 7)] * my_halo
        extra[3, rows, :] = depth_halo
        extra[4, rows, :] = my_halo
        return carry

    lax.fori_loop(0, 16, sweep_strips, 0)
    body_rows = pl.ds(TILE, rows_total)

    def sweep_back(i, carry):
        for k in range(4):
            p = i * 4 + k
            columns = (
                wide_star[p, pl.ds(2 * TILE, TILE), :],
                star_ref[p, pl.ds(2 * TILE, cols_total - 2 * TILE), :],
                wide_star[p, pl.ds(6 * TILE, TILE), :],
            )
            stack[p, body_rows, :] = jnp.concatenate(columns, axis=0).T
        return carry

    def sweep_extra(i, carry):
        for k in range(3):
            stack[STRIP + i * 3 + k, body_rows, :] = extra[i * 3 + k, inner, :].T
        return carry

    lax.fori_loop(0, 8, sweep_back, 0)
    lax.fori_loop(0, 3, sweep_extra, 0)

    def sweep_own(t, carry):
        start = pl.multiple_of(t * TILE, TILE)
        rows, here = pl.ds(start, TILE), pl.ds(start + TILE, TILE)
        my = my_ref[rows, :]
        depth = w_ref[0, rows, :]
        for l in range(1, LEVELS):
            depth = depth + w_ref[l, rows, :]
        stack[DEPTH, here, :] = depth.astype(F32)
        stack[METRIC, here, :] = my
        for l in range(LEVELS):
            stack[VM + l, here, :] = jnp.where(w_ref[l, rows, :] != 0, v_ref[l, rows, :], 0.0) * my
        all_edges(stack, edges, start + TILE)
        return carry

    def sweep_y(t, carry):
        r = pl.multiple_of(t * TILE + TILE, TILE)
        all_fluxes(stack, edges, fluxes, r, weights_to(advected, r, WY))
        all_updates(stack, fluxes, advected, r)
        return carry

    def copies(t_rows):
        return [
            pltpu.make_async_copy(out.at[pl.ds(f * LEVELS, LEVELS), t_rows, :], outs[f].at[:, t_rows, :], sems.at[f])
            for f in range(4)
        ]

    def sweep_out(t, carry):
        start = pl.multiple_of(t * TILE, TILE)
        rows = pl.ds(start, TILE)
        depth = stack[DEPTH, pl.ds(start + TILE, TILE), :]

        def put(p, x):
            out[p, rows, :] = x

        finish(
            advected, pl.multiple_of(start + TILE, TILE), depth,
            lambda i: stack[PLANES + i, pl.ds(start + TILE, TILE), :], lambda l: idf_ref[l, rows, :], coef_ref, put,
        )
        for copy in copies(rows):
            copy.start()
        return carry

    lax.fori_loop(0, tiles, sweep_own, 0)
    lax.fori_loop(0, tiles, sweep_y, 0)
    lax.fori_loop(1, tiles - 1, sweep_out, 0)
    for e, start in enumerate((0, rows_total - 2 * TILE)):
        adv_ref[:, pl.ds(e * 2 * TILE, 2 * TILE), :] = advected[:, pl.ds(start + TILE, 2 * TILE), :]
    for e, start in enumerate((0, rows_total - TILE)):
        weight_ref[e] = stack[pl.ds(PLANES, 4), pl.ds(start + TILE, TILE), :]
    for copy in copies(pl.ds(TILE, rows_total - 2 * TILE)):
        copy.wait()


def border_kernel(
    lat_ref, coef_ref, idf_lo, idf_hi, a_ref, b_ref, edge_ref, adv_ref, weight_ref, i0, i1, i2, i3,
    o0, o1, o2, o3,
    stack, edges, fluxes, advected, out, sems,
):
    outs = (o0, o1, o2, o3)
    rows_total = o0.shape[1]
    even = (lat_ref[0] & 1) == 0
    started = []
    for e in range(2):
        for p in range(PLANES):
            k = p // 2
            if e == 0:
                halo = jnp.where(even, b_ref[k], a_ref[k])
                stack[p, pl.ds(0, TILE), :] = turn(halo, 4) if p % 2 == 0 else halo
            else:
                halo = jnp.where(even, a_ref[k], b_ref[k])
                stack[p, pl.ds(2 * TILE, TILE), :] = halo if p % 2 == 0 else turn(halo, 4)
            stack[p, pl.ds(TILE, TILE), :] = edge_ref[e, p]
        advected[:, pl.ds(TILE if e == 0 else 0, 2 * TILE), :] = adv_ref[:, pl.ds(e * 2 * TILE, 2 * TILE), :]
        all_edges(stack, edges, 5 if e == 0 else 11)
        face = 6 if e == 0 else 12
        all_fluxes(stack, edges, fluxes, face, weights_to(advected, face, WY))
        all_updates(stack, fluxes, advected, 3 if e == 0 else 13)

        def put(p, x, e=e):
            out[e, p] = x

        idf = idf_lo if e == 0 else idf_hi
        finish(
            advected, TILE, stack[DEPTH, pl.ds(TILE, TILE), :],
            lambda p, e=e: weight_ref[e, p], lambda l, idf=idf: idf[l], coef_ref, put,
        )
        rows = pl.ds(0 if e == 0 else rows_total - TILE, TILE)
        for f in range(4):
            copy = pltpu.make_async_copy(
                out.at[e, pl.ds(f * LEVELS, LEVELS)], outs[f].at[:, rows, :], sems.at[e, f]
            )
            copy.start()
            started.append(copy)
    for copy in started:
        copy.wait()


def vmem(n):
    return [pl.BlockSpec(memory_space=pltpu.VMEM)] * n


def anywhere(n):
    return [pl.BlockSpec(memory_space=pl.ANY)] * n


def smem(n):
    return [pl.BlockSpec(memory_space=pltpu.SMEM)] * n


def shape(*dims):
    return jax.ShapeDtypeStruct(dims, F32)


PARAMS = pltpu.CompilerParams(vmem_limit_bytes=40 * 1024 * 1024)


def call_pack(base):
    rows, cols = base[5].shape
    steps = 2
    part = rows // steps
    wide = lambda: pl.BlockSpec((LEVELS, part, cols), lambda i: (0, i, 0))
    flat = lambda: pl.BlockSpec((rows, cols), lambda i: (0, 0))
    return pl.pallas_call(
        pack_kernel,
        grid=(steps,),
        out_shape=(shape(rows + 4 * TILE, LANES),) * 2,
        in_specs=[wide() for _ in range(5)] + [flat(), flat()],
        scratch_shapes=[pltpu.VMEM((rows, LANES), F32), pltpu.VMEM((3, TILE, LANES), F32)],
        out_specs=(
            pl.BlockSpec((rows + 4 * TILE, LANES), lambda i: (0, 0)),
            pl.BlockSpec((rows + 4 * TILE, LANES), lambda i: (0, 0)),
        ),
    )(*base)


def call_edge(lat_info, base, sides):
    return pl.pallas_call(
        edge_kernel,
        out_shape=(shape(PAIRS, TILE, LANES), shape(PAIRS, TILE, LANES), shape(2, 2 * PAIRS, TILE, LANES)),
        in_specs=smem(1) + vmem(9) + anywhere(1),
        out_specs=tuple(vmem(3)),
        compiler_params=PARAMS,
    )(lat_info, *base, *sides)


def call_flip(base):
    rows, cols = base[5].shape
    wide_rows = cols + 2 * TILE
    return pl.pallas_call(
        flip_kernel,
        out_shape=(shape(32, 4 * TILE, rows), shape(32, wide_rows, rows), shape(2, cols, rows)),
        in_specs=vmem(6),
        out_specs=tuple(vmem(3)),
        scratch_shapes=[
            pltpu.VMEM((STRIP, wide_rows, rows), F32),
            pltpu.VMEM((32, wide_rows, rows), F32),
            pltpu.VMEM((32, wide_rows, rows), F32),
        ],
        compiler_params=PARAMS,
        cost_estimate=pl.CostEstimate(flops=20_000_000, bytes_accessed=8_000_000, transcendentals=0),
    )(*base[:6])


def call_interior(spreading, brink, star, side, north, water, metric_y, diffusion, from_west, from_east):
    rows, cols = metric_y.shape
    stack_rows = rows + 2 * TILE
    wide_rows = cols + 4 * TILE
    return pl.pallas_call(
        interior_kernel,
        out_shape=(shape(LEVELS, rows, cols),) * 4 + (shape(AD_PLANES, 4 * TILE, LANES), shape(2, 4, TILE, LANES)),
        in_specs=smem(1) + vmem(9),
        out_specs=tuple(anywhere(4) + vmem(2)),
        scratch_shapes=[
            pltpu.VMEM((STRIP, 9 * TILE, rows), F32),
            pltpu.VMEM((34, stack_rows, LANES), F32),
            pltpu.VMEM((34, stack_rows, LANES), F32),
            pltpu.VMEM((32, 9 * TILE, rows), F32),
            pltpu.VMEM((2, wide_rows, rows), F32),
            pltpu.VMEM((9, wide_rows, rows), F32),
            pltpu.VMEM((32, TILE, rows), F32),
            pltpu.VMEM((PLANES + 4, stack_rows, LANES), F32),
            pltpu.VMEM((AD_PLANES, stack_rows, LANES), F32),
            pltpu.VMEM((32, rows, LANES), F32),
            pltpu.SemaphoreType.DMA((4,)),
        ],
        compiler_params=PARAMS,
    )(spreading, brink, star, side, north, water, metric_y, diffusion, from_west, from_east)


def call_border(lat_info, spreading, diffusion, got_a, got_b, edge, advected, weights, outs):
    _, rows, cols = outs[0].shape
    last = rows // TILE - 1
    return pl.pallas_call(
        border_kernel,
        grid=(1,),
        out_shape=(shape(LEVELS, rows, cols),) * 4,
        in_specs=smem(2)
        + [
            pl.BlockSpec((LEVELS - 1, TILE, cols), lambda i: (0, 0, 0)),
            pl.BlockSpec((LEVELS - 1, TILE, cols), lambda i: (0, last, 0)),
        ]
        + vmem(5)
        + anywhere(4),
        out_specs=tuple(anywhere(4)),
        scratch_shapes=[
            pltpu.VMEM((PLANES, 3 * TILE, LANES), F32),
            pltpu.VMEM((34, 3 * TILE, LANES), F32),
            pltpu.VMEM((34, 3 * TILE, LANES), F32),
            pltpu.VMEM((AD_PLANES, 3 * TILE, LANES), F32),
            pltpu.VMEM((2, 32, TILE, LANES), F32),
            pltpu.SemaphoreType.DMA((2, 4)),
        ],
        input_output_aliases={9 + f: f for f in range(4)},
        compiler_params=PARAMS,
    )(lat_info, spreading, diffusion, diffusion, got_a, got_b, edge, advected, weights, *outs)


def shards(heat, salt, east, north, water, metric_x, metric_y, diffusion, spreading, mirror):
    cols = metric_x.shape[1]
    lon_count, lat_count = lax.axis_size("lon"), lax.axis_size("lat")
    lon, lat = lax.axis_index("lon"), lax.axis_index("lat")
    lat_info = jnp.stack([lat, jnp.int32(lat_count)]).astype(jnp.int32)
    pivot = (mirror[0] // cols + lon) % lon_count

    base = (heat, salt, east, north, water, metric_x, metric_y)
    to_east, to_west = call_pack(base)
    ring = [(i, (i + 1) % lon_count) for i in range(lon_count)]
    from_west = lax.ppermute(to_east, "lon", ring)
    from_east = lax.ppermute(to_west, "lon", [(j, i) for i, j in ring])
    flipped = call_flip(base)
    sides = (from_west, from_east)
    rows_a, rows_b, edge = call_edge(lat_info, base, sides + (flipped[2],))

    index = lambda o, a: o * lat_count + a
    pairs = [(index(o, a), index(o, a ^ 1)) for o in range(lon_count) for a in range(lat_count)]
    got_a = lax.ppermute(rows_a, ("lon", "lat"), pairs)

    def across(k, x):
        fixed = []
        for o in range(lon_count):
            for a in range(1, lat_count - 1):
                fixed.append((index(o, a), index(o, ((a + 1) ^ 1) - 1)))
            fixed.append((index(o, lat_count - 1), index((k - o) % lon_count, lat_count - 1)))
        got = lax.ppermute(x, ("lon", "lat"), fixed)
        return got, interior(spreading, *flipped, north, water, metric_y, diffusion, from_west, from_east)

    interior = jax.jit(call_interior)
    got_b, results = lax.switch(pivot, [functools.partial(across, k) for k in range(lon_count)], rows_b)
    return call_border(lat_info, spreading, diffusion, got_a, got_b, edge, results[4], results[5], results[:4])


def solution(mesh):
    block = P(None, "lat", "lon")
    in_specs = (block,) * 5 + (P("lat", "lon"),) * 2 + (block, P(), P("lon"))
    return jax.shard_map(shards, mesh=mesh, in_specs=in_specs, out_specs=(block,) * 4, check_vma=False)
```
